32 devices in a mesh: dp: 8 (over y, x, core), band: 4 (over z).
Axes of the slice: x: 2, y: 2, z: 4, core: 2. Of those that a mesh axis runs over, the one named last changes fastest.
Arguments:
- latents: bfloat16 [32, 24, 24, 1536], P('dp', 'band'), may hold values from -13 to 13
- clip_text: bfloat16 [32, 77, 1280], P('dp'), may hold values from -6 to 6
- embedding: bfloat16 [32, 64], P('dp'), may hold values from -6 to 6
- lengths: int32 [32], P('dp'), may hold values from 5 to 77, as said below
- conv_weight: bfloat16 [9, 1536], P(None, ('dp', 'band')), may hold values from -2 to 2
- up_weight: bfloat16 [1536, 6144], P(('dp', 'band')), may hold values from -0.15625 to 0.15625
- down_weight: bfloat16 [6144, 1536], P(('dp', 'band')), may hold values from -0.078125 to 0.078125
- hidden_vecs: bfloat16 [3, 6144], P(None, ('dp', 'band')), may hold values from -3 to 3
- vectors: bfloat16 [8, 1536], P(None, ('dp', 'band')), may hold values from -2 to 2
- time_weight: bfloat16 [64, 3072], P(None, ('dp', 'band')), may hold values from -0.375 to 0.375
- map_weight: bfloat16 [1280, 1536], P(('dp', 'band')), may hold values from -0.15625 to 0.15625
- attn_in: bfloat16 [3, 1536, 1536], P(None, ('dp', 'band')), may hold values from -0.15625 to 0.15625
- out_weight: bfloat16 [1536, 1536], P(('dp', 'band')), may hold values from -1.25 to 1.25
- grad_out: bfloat16 [32, 24, 24, 1536], P('dp', 'band'), may hold values from -6 to 6
Outputs:
- layer_out: bfloat16 [32, 24, 24, 1536], P('dp', 'band')
- latent_grad: bfloat16 [32, 24, 24, 1536], P('dp', 'band')
- text_grad: bfloat16 [32, 77, 1280], P('dp', None, 'band')
- conv_grad: float32 [9, 1536], P(None, ('dp', 'band'))
- up_grad: float32 [1536, 6144], P(('dp', 'band'))
- down_grad: float32 [6144, 1536], P(('dp', 'band'))
- hidden_grad: float32 [3, 6144], P(None, ('dp', 'band'))
- vector_grad: float32 [8, 1536], P(None, ('dp', 'band'))
- time_grad: float32 [64, 3072], P(None, ('dp', 'band'))
- map_grad: float32 [1280, 1536], P(('dp', 'band'))
- attn_grad: float32 [3, 1536, 1536], P(None, ('dp', 'band'))
- out_grad: float32 [1536, 1536], P(('dp', 'band'))
The draws below stay inside these ranges and needn't reach their ends.
Inputs may be any that keep to these rules, and one draw needn't show every extreme that they name: `lengths`: in every draw some latent uses all 77 text tokens and another uses 5.
All inputs are finite; a program needn't handle non-finite values.
Results may differ from the reference program's by a relative error of at most 0.024.
Values may be sent and summed in bfloat16 or wider, within the bound.
A program may use at most 448 MiB of HBM per device.

```python
import jax
import jax.numpy as jnp
from jax import lax

C = 1536
HEADS = 24
HEAD_DIM = 64
INNER = 6144
CLIP = 1280
R = 64
TEXT = 77
HEIGHT = 24
WIDTH = 24
LATENTS = 32


def draw_latents(key, part):
    noise_key, pattern_key = jax.random.split(key)
    slope = jnp.arange(HEIGHT, dtype=jnp.float32).reshape(1, HEIGHT, 1, 1) * (2.0 / (HEIGHT - 1))
    pattern = jax.random.truncated_normal(pattern_key, -3.0, 3.0, (LATENTS, 1, 1, C), jnp.float32)
    noise = jax.random.truncated_normal(noise_key, -4.0, 4.0, (LATENTS, HEIGHT, WIDTH, C), jnp.float32)
    return (noise + slope * pattern).astype(jnp.bfloat16)


def draw_lengths(key, part):
    subkeys = jax.random.split(key, 3)
    values = jax.random.randint(subkeys[0], (LATENTS,), 5, TEXT + 1)
    longest = jax.random.randint(subkeys[1], (), 0, LATENTS)
    stride = jax.random.randint(subkeys[2], (), 1, LATENTS)
    shortest = (longest + stride) % LATENTS
    values = values.at[longest].set(TEXT)
    values = values.at[shortest].set(5)
    return values.astype(jnp.int32)


def block_levels(key, shape, cuts, smallest, largest):
    loudness = 1.0
    for axis_at, blocks in cuts:
        steps = jax.random.uniform(jax.random.fold_in(jax.random.fold_in(key, 6), axis_at), (blocks,), jnp.float32, smallest / len(cuts), largest / len(cuts))
        loudness = loudness * jnp.repeat(jnp.exp(steps), shape[axis_at] // blocks).reshape((-1,) + (1,) * (len(shape) - 1 - axis_at))
    return loudness


def bell_draw(stream_key, extent, scale, limit, cuts=(), held_as=jnp.bfloat16):
    values = jax.random.normal(stream_key, extent, jnp.float32) * scale
    if len(cuts) > 0:
        values = block_levels(stream_key, extent, cuts, -0.22, 0.18) * values
    return jnp.clip(values, min=-limit, max=limit).astype(held_as)


def setup_inputs(seed: int = 0) -> dict:
    streams_of = jax.random.split(jax.random.key(seed), 15)
    return {
        "latents": draw_latents(jax.random.fold_in(streams_of[14], 71), 0),
        "clip_text": bell_draw(streams_of[1], (LATENTS, TEXT, CLIP), 1.0, 6.0, ((0, 8),)),
        "embedding": bell_draw(streams_of[2], (LATENTS, R), 1.0, 6.0, ((0, 8),)),
        "lengths": draw_lengths(jax.random.fold_in(streams_of[14], 71), 0),
        "conv_weight": bell_draw(streams_of[4], (9, C), 9 ** -0.5, 2.0, ((1, 32),)),
        "up_weight": bell_draw(streams_of[5], (C, INNER), C ** -0.5, 0.15625, ((0, 32),)),
        "down_weight": bell_draw(streams_of[6], (INNER, C), INNER ** -0.5, 0.078125, ((0, 32),)),
        "hidden_vecs": bell_draw(streams_of[7], (3, INNER), 0.5, 3.0, ((1, 32),)),
        "vectors": bell_draw(streams_of[8], (8, C), 0.3, 2.0, ((1, 32),)),
        "time_weight": bell_draw(streams_of[9], (R, 2 * C), (4 * R) ** -0.5, 0.375, ((1, 32),)),
        "map_weight": bell_draw(streams_of[10], (CLIP, C), CLIP ** -0.5, 0.15625, ((0, 32),)),
        "attn_in": bell_draw(streams_of[11], (3, C, C), C ** -0.5, 0.15625, ((1, 32),)),
        "out_weight": bell_draw(streams_of[12], (C, C), (max(1, C * 8 // (HEIGHT * WIDTH))) ** -0.5, 1.25, ((0, 32),)),
        "grad_out": bell_draw(streams_of[13], (LATENTS, HEIGHT, WIDTH, C), 1.0, 6.0, ((0, 8), (1, 4))),
    }


@jax.custom_vjp
def low(v):
    return lax.optimization_barrier(v.astype(jnp.bfloat16)).astype(jnp.float32)

@jax.custom_vjp
def low_back(v):
    return v

def low_keep(v):
    return (low(v), None)

def low_pass(kept, grad):
    return (grad,)

def back_keep(v):
    return (v, None)

def back_low(kept, grad):
    return (low(grad),)
low.defvjp(low_keep, low_pass)
low_back.defvjp(back_keep, back_low)

def rounded(array_in):
    return low_back(low(array_in))

def product(left_op, right_op):
    return jnp.dot(left_op, right_op, precision=lax.Precision.HIGHEST, preferred_element_type=jnp.float32)

def layer_norm(array_in):
    center = array_in - lax.optimization_barrier(jnp.mean(array_in, axis=-1, keepdims=True))
    spread = lax.optimization_barrier(jnp.mean(center * center, axis=-1, keepdims=True))
    return center * lax.rsqrt(spread + 1e-06)

def forward_one(latent, clip_words, embedding, length, conv_weight, up_weight, down_weight, hidden_vecs, vectors, time_weight, map_weight, attn_in, out_weight):
    pixels = HEIGHT * WIDTH
    framed = jnp.pad(latent, ((1, 1), (1, 1), (0, 0)))
    conv_out = jnp.broadcast_to(vectors[0], latent.shape)
    for offset in range(9):
        row_shift = offset // 3
        col_shift = offset % 3
        conv_out = conv_out + conv_weight[offset] * framed[row_shift:row_shift + HEIGHT, col_shift:col_shift + WIDTH]
    conv_out = low_back(conv_out)
    first_in = low(layer_norm(conv_out.reshape(pixels, C)))
    up_out = low_back(product(first_in, up_weight) + hidden_vecs[0])
    active = jax.nn.gelu(up_out, approximate=False)
    strength = jnp.sqrt(lax.optimization_barrier(jnp.sum(active * active, axis=0)))
    grn_ratio = strength / (jnp.mean(strength) + 1e-06)
    grn_out = low(hidden_vecs[1] * (active * grn_ratio) + hidden_vecs[2] + active)
    lowered = low_back(product(grn_out, down_weight) + vectors[1])
    first_sum = latent.reshape(pixels, C) + lowered
    modulation = product(embedding[None, :], time_weight)[0]
    scale_vec = modulation[:C] + vectors[2]
    shift_vec = modulation[C:] + vectors[3]
    second = first_sum * (1.0 + scale_vec) + shift_vec
    second_in = low(layer_norm(second))
    mapped = rounded(product(low(jax.nn.silu(clip_words)), map_weight) + vectors[4])
    sources = jnp.concatenate([second_in, mapped], axis=0)
    query_rows = rounded(product(second_in, attn_in[0]) + vectors[5]).reshape(pixels, HEADS, HEAD_DIM)
    key_rows = rounded(product(sources, attn_in[1])).reshape(pixels + TEXT, HEADS, HEAD_DIM)
    value_rows = rounded(product(sources, attn_in[2]) + vectors[6]).reshape(pixels + TEXT, HEADS, HEAD_DIM)
    scores = low_back(jnp.einsum('qhd,khd->hqk', query_rows, key_rows, precision=lax.Precision.HIGHEST) * HEAD_DIM ** (-0.5))
    places = jnp.arange(pixels + TEXT, dtype=jnp.int32)
    valid_keys = places < pixels + length
    scores = jnp.where(valid_keys[None, None, :], scores, -1000000000.0)
    weights = jax.nn.softmax(scores, axis=-1)
    mixed_out = jnp.einsum('hqk,khd->qhd', low(weights), value_rows, precision=lax.Precision.HIGHEST)
    mixed_out = rounded(mixed_out.reshape(pixels, C))
    attended = low_back(product(mixed_out, out_weight) + vectors[7])
    return (second + attended).reshape(HEIGHT, WIDTH, C)

def reference(latents, clip_text, embedding, lengths, conv_weight, up_weight, down_weight, hidden_vecs, vectors, time_weight, map_weight, attn_in, out_weight, grad_out):
    params = tuple((element.astype(jnp.float32) for element in (conv_weight, up_weight, down_weight, hidden_vecs, vectors, time_weight, map_weight, attn_in, out_weight)))

    def one_latent(running, inputs):
        latent, clip_words, embed_row, length, cotangent = inputs

        def forward_at(latent_in, words_in, *weights_in):
            return forward_one(latent_in, words_in, embed_row, length, *weights_in)
        result, pullback = jax.vjp(forward_at, latent, clip_words, *params)
        grads_all = pullback(cotangent)
        running = tuple((earlier + addend for earlier, addend in zip(running, grads_all[2:])))
        return (running, (result.astype(jnp.bfloat16), grads_all[0].astype(jnp.bfloat16), grads_all[1].astype(jnp.bfloat16)))
    initial = tuple((jnp.zeros(element.shape, jnp.float32) for element in params))
    totals, outputs = lax.scan(one_latent, initial, (latents.astype(jnp.float32), clip_text.astype(jnp.float32), embedding.astype(jnp.float32), lengths, grad_out.astype(jnp.float32)))
    return (outputs[0], outputs[1], outputs[2], totals[0], totals[1], totals[2], totals[3], totals[4], totals[5], totals[6], totals[7], totals[8])
```

```python
import jax
import jax.numpy as jnp
from jax import lax
from jax.sharding import PartitionSpec as P

HEAD_DIM = 64


def with_halo(array, sides, width):
    for axis, dim in sides:
        size, length = (lax.axis_size(axis), array.shape[dim])
        up = [(i, (i + 1) % size) for i in range(size - 1)]
        down = [(j, i) for i, j in up]
        last = lax.slice_in_dim(array, length - width, length, axis=dim)
        first = lax.slice_in_dim(array, 0, width, axis=dim)
        before = lax.ppermute(last, axis, up)
        after = lax.ppermute(first, axis, down)
        array = jnp.concatenate([before, array, after], axis=dim)
    return array


def product(left_op, right_op):
    return jnp.dot(left_op, right_op, preferred_element_type=jnp.float32)


def product_tn(left_op, right_op):
    return lax.dot_general(
        left_op, right_op, (((0,), (0,)), ((), ())), preferred_element_type=jnp.float32
    )


def product_nt(left_op, right_op):
    return lax.dot_general(
        left_op, right_op, (((1,), (1,)), ((), ())), preferred_element_type=jnp.float32
    )


def norm_parts(array_in):
    center = array_in - jnp.mean(array_in, axis=-1, keepdims=True)
    spread = jnp.mean(center * center, axis=-1, keepdims=True)
    inverse = lax.rsqrt(spread + 1e-06)
    return (center * inverse, inverse)


def norm_back(incoming, normed, inverse):
    return inverse * (
        incoming
        - jnp.mean(incoming, axis=-1, keepdims=True)
        - normed * jnp.mean(incoming * normed, axis=-1, keepdims=True)
    )


def column_sums(array_in):
    return jnp.sum(array_in.astype(jnp.float32), axis=0)


def gelu_exact(array_in):
    return jax.nn.gelu(array_in, approximate=False)


def masked_scores(query_one, key_one, valid_one):
    raw_scores = jnp.einsum(
        "qhd,khd->hqk", query_one, key_one, preferred_element_type=jnp.float32
    ) * HEAD_DIM ** (-0.5)
    return jnp.where(valid_one[None, None, :], raw_scores, -1000000000.0)


def attend_one(items):
    query_one, key_one, value_one, valid_one = items
    scores = masked_scores(query_one, key_one, valid_one)
    top_score = jnp.max(scores, axis=-1, keepdims=True)
    exponent = jnp.exp(scores - top_score)
    row_total = jnp.sum(exponent, axis=-1, keepdims=True)
    log_total = top_score + jnp.log(row_total)
    probs_low = (exponent / row_total).astype(jnp.bfloat16)
    mixed_one = jnp.einsum(
        "hqk,khd->qhd", probs_low, value_one, preferred_element_type=jnp.float32
    ).astype(jnp.bfloat16)
    return (mixed_one, log_total)


def attend_back(items):
    query_one, key_one, value_one, valid_one, log_one, gmix_one = items
    weights_again = jnp.exp(masked_scores(query_one, key_one, valid_one) - log_one)
    g_probs = jnp.einsum("qhd,khd->hqk", gmix_one, value_one, preferred_element_type=jnp.float32)
    inner_sum = jnp.sum(weights_again * g_probs, axis=-1, keepdims=True)
    g_score = (weights_again * (g_probs - inner_sum)).astype(jnp.bfloat16)
    probs_again = weights_again.astype(jnp.bfloat16)
    g_query = (
        jnp.einsum("hqk,khd->qhd", g_score, key_one, preferred_element_type=jnp.float32)
        * HEAD_DIM ** (-0.5)
    ).astype(jnp.bfloat16)
    g_key = jnp.einsum(
        "hqk,qhd->khd", g_score, query_one, preferred_element_type=jnp.float32
    ) * HEAD_DIM ** (-0.5)
    g_value = jnp.einsum("hqk,qhd->khd", probs_again, gmix_one, preferred_element_type=jnp.float32)
    return (g_query, g_key, g_value)


def per_device(
    latents,
    clip_text,
    embedding,
    lengths,
    conv_weight,
    up_weight,
    down_weight,
    hidden_vecs,
    vectors,
    time_weight,
    map_weight,
    attn_in,
    out_weight,
    grad_out,
):
    lat_count, band_rows, columns, channels = latents.shape
    tokens_lat = band_rows * columns
    tok_rows = lat_count * tokens_lat
    hidden_width = up_weight.shape[1]
    text_len = clip_text.shape[1]
    clip_width = clip_text.shape[2]
    band_size = lax.axis_size("band")
    band_index = lax.axis_index("band")
    pixel_count = tokens_lat * band_size
    head_count = channels // HEAD_DIM
    band_share = 1.0 / band_size
    res_shards = (conv_weight, up_weight, down_weight, hidden_vecs, vectors)
    attn_shards = (time_weight, map_weight, attn_in, out_weight)
    res_full = (
        lax.all_gather(res_shards[0], ("dp", "band"), axis=1, tiled=True),
        lax.all_gather(res_shards[1], ("dp", "band"), axis=0, tiled=True),
        lax.all_gather(res_shards[2], ("dp", "band"), axis=0, tiled=True),
        lax.all_gather(res_shards[3], ("dp", "band"), axis=1, tiled=True),
        lax.all_gather(res_shards[4], ("dp", "band"), axis=1, tiled=True),
    )
    attn_full = (
        lax.all_gather(attn_shards[0], ("dp", "band"), axis=1, tiled=True),
        lax.all_gather(attn_shards[1], ("dp", "band"), axis=0, tiled=True),
        lax.all_gather(attn_shards[2], ("dp", "band"), axis=1, tiled=True),
        lax.all_gather(attn_shards[3], ("dp", "band"), axis=0, tiled=True),
    )
    hidden_values = res_full[3].astype(jnp.float32)
    vec_values = res_full[4].astype(jnp.float32)
    framed = with_halo(latents, (("band", 1),), 1)
    framed = jnp.pad(framed, ((0, 0), (0, 0), (1, 1), (0, 0)))
    conv_taps = res_full[0].astype(jnp.float32)
    conv_out = jnp.broadcast_to(vec_values[0], latents.shape)
    for offset in range(9):
        row_shift = offset // 3
        col_shift = offset % 3
        conv_out = conv_out + conv_taps[offset] * framed[
            :, row_shift : row_shift + band_rows, col_shift : col_shift + columns
        ].astype(jnp.float32)
    first_norm, first_inv = norm_parts(conv_out.reshape(tok_rows, channels))
    first_in = first_norm.astype(jnp.bfloat16)
    up_out = product(first_in, res_full[1]) + hidden_values[0]
    active = gelu_exact(up_out)
    active_lat = active.reshape(lat_count, tokens_lat, hidden_width)
    square_sums = lax.psum(
        jnp.sum(active_lat * active_lat, axis=1).astype(jnp.bfloat16), "band"
    ).astype(jnp.float32)
    strength = jnp.sqrt(square_sums)
    grn_denom = jnp.mean(strength, axis=-1, keepdims=True) + 1e-06
    grn_ratio = strength / grn_denom
    gamma_vec = hidden_values[1]
    grn_out = (
        (gamma_vec * (active_lat * grn_ratio[:, None]) + hidden_values[2] + active_lat)
        .astype(jnp.bfloat16)
        .reshape(tok_rows, hidden_width)
    )
    first_sum = latents.reshape(tok_rows, channels).astype(jnp.float32) + (
        product(grn_out, res_full[2]) + vec_values[1]
    )
    modulation = product(embedding, attn_full[0])
    scale_vec = modulation[:, :channels] + vec_values[2]
    shift_vec = modulation[:, channels:] + vec_values[3]
    first_lat = first_sum.reshape(lat_count, tokens_lat, channels)
    second = first_lat * (1.0 + scale_vec[:, None]) + shift_vec[:, None]
    second_norm, second_inv = norm_parts(second)
    second_in = second_norm.astype(jnp.bfloat16).reshape(tok_rows, channels)
    clip_words = (
        jax.nn.silu(clip_text.astype(jnp.float32))
        .astype(jnp.bfloat16)
        .reshape(lat_count * text_len, clip_width)
    )
    mapped = (product(clip_words, attn_full[1]) + vec_values[4]).astype(jnp.bfloat16)
    projections = attn_full[2]
    query_rows = (product(second_in, projections[0]) + vec_values[5]).astype(jnp.bfloat16)
    pixel_key = (
        product(second_in, projections[1])
        .astype(jnp.bfloat16)
        .reshape(lat_count, tokens_lat, channels)
    )
    pixel_value = (
        (product(second_in, projections[2]) + vec_values[6])
        .astype(jnp.bfloat16)
        .reshape(lat_count, tokens_lat, channels)
    )
    all_key, all_value = (
        lax.all_gather(pixel_key, "band", axis=1, tiled=True),
        lax.all_gather(pixel_value, "band", axis=1, tiled=True),
    )
    text_key = (
        product(mapped, projections[1]).astype(jnp.bfloat16).reshape(lat_count, text_len, channels)
    )
    text_value = (
        (product(mapped, projections[2]) + vec_values[6])
        .astype(jnp.bfloat16)
        .reshape(lat_count, text_len, channels)
    )
    key_rows = jnp.concatenate([all_key, text_key], axis=1).reshape(
        lat_count, pixel_count + text_len, head_count, HEAD_DIM
    )
    value_rows = jnp.concatenate([all_value, text_value], axis=1).reshape(
        lat_count, pixel_count + text_len, head_count, HEAD_DIM
    )
    query_heads = query_rows.reshape(lat_count, tokens_lat, head_count, HEAD_DIM)
    key_places = jnp.arange(pixel_count + text_len, dtype=jnp.int32)
    valid_keys = key_places[None, :] < pixel_count + lengths[:, None]
    mixed_heads, log_totals = lax.map(attend_one, (query_heads, key_rows, value_rows, valid_keys))
    mixed_out = mixed_heads.reshape(tok_rows, channels)
    attended = product(mixed_out, attn_full[3]) + vec_values[7]
    layer_out = (
        (second.reshape(tok_rows, channels) + attended).astype(jnp.bfloat16).reshape(latents.shape)
    )
    res_back = (
        lax.all_gather(res_shards[0], ("dp", "band"), axis=1, tiled=True),
        lax.all_gather(res_shards[1], ("dp", "band"), axis=0, tiled=True),
        lax.all_gather(res_shards[2], ("dp", "band"), axis=0, tiled=True),
        lax.all_gather(res_shards[3], ("dp", "band"), axis=1, tiled=True),
        lax.all_gather(res_shards[4], ("dp", "band"), axis=1, tiled=True),
    )
    attn_back = (
        lax.all_gather(attn_shards[0], ("dp", "band"), axis=1, tiled=True),
        lax.all_gather(attn_shards[1], ("dp", "band"), axis=0, tiled=True),
        lax.all_gather(attn_shards[2], ("dp", "band"), axis=1, tiled=True),
        lax.all_gather(attn_shards[3], ("dp", "band"), axis=0, tiled=True),
    )
    proj_back = attn_back[2]
    grad_rows = grad_out.reshape(tok_rows, channels)
    grad_float = grad_rows.astype(jnp.float32)
    out_grad_w = product_tn(mixed_out, grad_rows)
    g_mixed = (
        product_nt(grad_rows, attn_back[3])
        .astype(jnp.bfloat16)
        .reshape(lat_count, tokens_lat, head_count, HEAD_DIM)
    )
    g_query_heads, g_key, g_value = lax.map(
        attend_back, (query_heads, key_rows, value_rows, valid_keys, log_totals, g_mixed)
    )
    g_query = g_query_heads.reshape(tok_rows, channels)
    g_key = g_key.reshape(lat_count, pixel_count + text_len, channels)
    g_value = g_value.reshape(lat_count, pixel_count + text_len, channels)
    pixel_gkey, pixel_gvalue = (
        lax.psum_scatter(
            g_key[:, :pixel_count].astype(jnp.bfloat16), "band", scatter_dimension=1, tiled=True
        ).astype(jnp.float32),
        lax.psum_scatter(
            g_value[:, :pixel_count].astype(jnp.bfloat16), "band", scatter_dimension=1, tiled=True
        ).astype(jnp.float32),
    )
    text_gkey, text_gvalue = (
        lax.psum(g_key[:, pixel_count:].astype(jnp.bfloat16), "band").astype(jnp.float32),
        lax.psum(g_value[:, pixel_count:].astype(jnp.bfloat16), "band").astype(jnp.float32),
    )
    pixel_kb = pixel_gkey.astype(jnp.bfloat16).reshape(tok_rows, channels)
    pixel_vb = pixel_gvalue.astype(jnp.bfloat16).reshape(tok_rows, channels)
    text_kb = text_gkey.astype(jnp.bfloat16).reshape(lat_count * text_len, channels)
    text_vb = text_gvalue.astype(jnp.bfloat16).reshape(lat_count * text_len, channels)
    g_second_in = (
        product_nt(g_query, proj_back[0])
        + product_nt(pixel_kb, proj_back[1])
        + product_nt(pixel_vb, proj_back[2])
    )
    grad_query_w = product_tn(second_in, g_query)
    grad_key_w = product_tn(second_in, pixel_kb) + band_share * product_tn(mapped, text_kb)
    grad_value_w = product_tn(second_in, pixel_vb) + band_share * product_tn(mapped, text_vb)
    g_mapped = (product_nt(text_kb, proj_back[1]) + product_nt(text_vb, proj_back[2])).astype(
        jnp.bfloat16
    )
    grad_map_w = band_share * product_tn(clip_words, g_mapped)
    clip_slice = clip_width // band_size
    map_rows = lax.dynamic_slice_in_dim(attn_back[1], band_index * clip_slice, clip_slice, 0)
    text_part = lax.dynamic_slice_in_dim(clip_text, band_index * clip_slice, clip_slice, 2).astype(
        jnp.float32
    )
    sigmoid_text = jax.nn.sigmoid(text_part)
    g_words = product_nt(g_mapped, map_rows).reshape(lat_count, text_len, clip_slice)
    text_grad = (g_words * (sigmoid_text * (1.0 + text_part * (1.0 - sigmoid_text)))).astype(
        jnp.bfloat16
    )
    g_second = grad_float.reshape(lat_count, tokens_lat, channels) + norm_back(
        g_second_in.reshape(lat_count, tokens_lat, channels), second_norm, second_inv
    )
    g_scale = jnp.sum(g_second * first_lat, axis=1)
    g_shift = jnp.sum(g_second, axis=1)
    grad_time_w = lax.dot_general(
        embedding.astype(jnp.float32),
        jnp.concatenate([g_scale, g_shift], axis=1),
        (((0,), (0,)), ((), ())),
        precision=lax.Precision.HIGHEST,
        preferred_element_type=jnp.float32,
    )
    attn_grads = (
        lax.psum_scatter(grad_time_w, ("dp", "band"), scatter_dimension=1, tiled=True),
        lax.psum_scatter(grad_map_w, ("dp", "band"), scatter_dimension=0, tiled=True),
        lax.psum_scatter(
            jnp.stack([grad_query_w, grad_key_w, grad_value_w]),
            ("dp", "band"),
            scatter_dimension=1,
            tiled=True,
        ),
        lax.psum_scatter(out_grad_w, ("dp", "band"), scatter_dimension=0, tiled=True),
    )
    g_first = g_second * (1.0 + scale_vec[:, None])
    g_down = g_first.astype(jnp.bfloat16).reshape(tok_rows, channels)
    grad_down_w = product_tn(grn_out, g_down)
    g_grn = product_nt(g_down, res_back[2]).reshape(lat_count, tokens_lat, hidden_width)
    grad_gamma = jnp.sum(g_grn * active_lat * grn_ratio[:, None], axis=(0, 1))
    grad_beta = jnp.sum(g_grn, axis=(0, 1))
    g_ratio = lax.psum(
        jnp.sum(g_grn * gamma_vec * active_lat, axis=1).astype(jnp.bfloat16), "band"
    ).astype(jnp.float32)
    g_strength = g_ratio / grn_denom - jnp.sum(g_ratio * strength, axis=-1, keepdims=True) / (
        hidden_width * grn_denom * grn_denom
    )
    g_active = (
        g_grn * (1.0 + gamma_vec * grn_ratio[:, None])
        + active_lat * (g_strength / strength)[:, None]
    )
    gelu_value, gelu_pull = jax.vjp(gelu_exact, up_out)
    g_up = gelu_pull(g_active.reshape(tok_rows, hidden_width))[0].astype(jnp.bfloat16)
    grad_up_w = product_tn(first_in, g_up)
    g_conv = (
        norm_back(product_nt(g_up, res_back[1]), first_norm, first_inv)
        .astype(jnp.bfloat16)
        .reshape(latents.shape)
    )
    g_framed = with_halo(g_conv, (("band", 1),), 1)
    g_framed = jnp.pad(g_framed, ((0, 0), (0, 0), (1, 1), (0, 0)))
    conv_back = res_back[0].astype(jnp.float32)
    g_conv_f = g_conv.astype(jnp.float32)
    back_sum = g_first.reshape(latents.shape)
    tap_grads = []
    for offset in range(9):
        row_shift = offset // 3
        col_shift = offset % 3
        window = framed[
            :, row_shift : row_shift + band_rows, col_shift : col_shift + columns
        ].astype(jnp.float32)
        tap_grads.append(jnp.sum(g_conv_f * window, axis=(0, 1, 2)))
        back_sum = back_sum + conv_back[offset] * g_framed[
            :, 2 - row_shift : 2 - row_shift + band_rows, 2 - col_shift : 2 - col_shift + columns
        ].astype(jnp.float32)
    latent_grad = back_sum.astype(jnp.bfloat16)
    grad_vectors = jnp.stack(
        [
            jnp.sum(g_conv_f, axis=(0, 1, 2)),
            column_sums(g_down),
            jnp.sum(g_scale, axis=0),
            jnp.sum(g_shift, axis=0),
            band_share * column_sums(g_mapped),
            column_sums(g_query),
            column_sums(pixel_vb) + band_share * column_sums(text_vb),
            jnp.sum(grad_float, axis=0),
        ]
    )
    grad_hidden = jnp.stack([column_sums(g_up), grad_gamma, grad_beta])
    grad_conv_w = jnp.stack(tap_grads)
    res_grads = (
        lax.psum_scatter(grad_conv_w, ("dp", "band"), scatter_dimension=1, tiled=True),
        lax.psum_scatter(grad_up_w, ("dp", "band"), scatter_dimension=0, tiled=True),
        lax.psum_scatter(grad_down_w, ("dp", "band"), scatter_dimension=0, tiled=True),
        lax.psum_scatter(grad_hidden, ("dp", "band"), scatter_dimension=1, tiled=True),
        lax.psum_scatter(grad_vectors, ("dp", "band"), scatter_dimension=1, tiled=True),
    )
    return (
        layer_out,
        latent_grad,
        text_grad,
        res_grads[0],
        res_grads[1],
        res_grads[2],
        res_grads[3],
        res_grads[4],
        attn_grads[0],
        attn_grads[1],
        attn_grads[2],
        attn_grads[3],
    )


PLANE = 4
LINE = 4


def swap(value, bit):
    return lax.ppermute(value, "dp", [(i, i ^ bit) for i in range(2 * PLANE)])


def rotate(value, step):
    return lax.ppermute(value, "band", [(i, (i + step) % LINE) for i in range(LINE)])


def pick(value, index, axis=0):
    return lax.dynamic_index_in_dim(value, index, axis, keepdims=False)


def put(buffer, value, index, axis=0):
    return lax.dynamic_update_index_in_dim(buffer, value, index, axis)


def spread_line(blocks, place):
    result = jnp.zeros(blocks.shape, blocks.dtype)
    result = put(result, pick(blocks, place), place)
    for step in range(1, LINE):
        moved = rotate(pick(blocks, (place + step) % LINE), step)
        result = put(result, moved, (place - step) % LINE)
    return result


def gather_line(shard, place):
    parts, rows, cols = shard.shape
    result = jnp.zeros((parts, LINE, rows, cols), shard.dtype)
    result = put(result, shard, place, 1)
    for step in range(1, LINE):
        result = put(result, rotate(shard, step), (place - step) % LINE, 1)
    return result


def gather_plane(block, plane):
    rows, cols = block.shape
    half = rows // 2
    by_x, by_y = (swap(block, 2), swap(block, 4))
    upper = swap(by_y[:half], 2)
    lower = swap(by_x[half:], 4)
    result = jnp.zeros((PLANE, rows, cols), block.dtype)
    result = put(result, block, plane)
    result = put(result, by_x, plane ^ 1)
    result = put(result, by_y, plane ^ 2)
    zero = jnp.int32(0)
    result = lax.dynamic_update_slice(result, upper[None], (plane ^ 3, zero, zero))
    result = lax.dynamic_update_slice(result, lower[None], (plane ^ 3, zero + half, zero))
    return (result, (by_x, by_y))


def gather_all(shards, plane, place):
    results = []
    line_done, plane_done = (None, None)
    for shard in shards:
        if line_done is not None:
            shard, _ = lax.optimization_barrier((shard, line_done))
        parts, rows, cols = shard.shape
        line = gather_line(shard, place).reshape(parts * LINE * rows, cols)
        line_done = line
        if plane_done is not None:
            line, _ = lax.optimization_barrier((line, plane_done))
        full, plane_done = gather_plane(line, plane)
        results.append(full.reshape(PLANE * parts * LINE * rows, cols))
    return results


def reduce_owner(piece, parts, plane, place):
    low = jnp.bfloat16
    far = [piece(plane ^ 3, half).astype(low) for half in range(2)]
    via_x, via_y = (swap(far[0], 2), swap(far[1], 4))
    out_x = [piece(plane ^ 1, 0).astype(low), None]
    out_y = [None, piece(plane ^ 2, 1).astype(low)]
    got_x, got_y = ([swap(out_x[0], 2), None], [None, swap(out_y[1], 4)])
    out_x[1] = (piece(plane ^ 1, 1) + via_y.astype(jnp.float32)).astype(low)
    out_y[0] = (piece(plane ^ 2, 0) + via_x.astype(jnp.float32)).astype(low)
    got_x[1], got_y[0] = (swap(out_x[1], 2), swap(out_y[0], 4))
    results = []
    for half in range(2):
        total = (
            piece(plane, half)
            + got_x[half].astype(jnp.float32)
            + got_y[half].astype(jnp.float32)
        )
        rows, cols = total.shape
        total = total.reshape(parts, LINE, rows // (parts * LINE), cols)
        summed = pick(total, place, 1)
        for step in range(1, LINE):
            sent = pick(total, (place + step) % LINE, 1).astype(low)
            summed = summed + rotate(sent, step).astype(jnp.float32)
        results.append(summed)
    return jnp.concatenate(results, axis=-1)


def gather_small(value, plane, core, place):
    cores = jnp.zeros((2,) + value.shape, value.dtype)
    cores = put(put(cores, value, core), swap(value, 1), 1 - core)
    line = jnp.zeros((2, LINE) + value.shape, value.dtype)
    line = put(line, cores, place, 1)
    for step in range(1, LINE):
        line = put(line, rotate(cores, step), (place - step) % LINE, 1)
    return gather_small_plane(line, plane)


def gather_small_line(value, plane, place):
    line = jnp.zeros((LINE,) + value.shape, value.dtype)
    line = put(line, value, place)
    for step in range(1, LINE):
        line = put(line, rotate(value, step), (place - step) % LINE)
    return gather_small_plane(line, plane)


def gather_small_plane(line, plane):
    by_x = swap(line, 2)
    both = jnp.stack([line, by_x])
    by_y = swap(both, 4)
    full = jnp.zeros((PLANE,) + line.shape, line.dtype)
    full = put(put(full, line, plane), by_x, plane ^ 1)
    return put(put(full, by_y[0], plane ^ 2), by_y[1], plane ^ 3)


def reduce_small(value, plane, place):
    both = jnp.stack([pick(value, plane ^ 1), pick(value, plane ^ 3)])
    by_x = swap(both, 2)
    mine = pick(value, plane) + by_x[0]
    other = pick(value, plane ^ 2) + by_x[1]
    mine = mine + swap(other, 4)
    summed = pick(mine, place)
    for step in range(1, LINE):
        summed = summed + rotate(pick(mine, (place + step) % LINE), step)
    return summed


def pair(value):
    return jnp.stack([value, swap(value, 1)])


def pair_sum(value):
    return value + swap(value, 1)[::-1]


def own_sum(own, partner):
    return own + swap(partner.astype(jnp.bfloat16), 1).astype(jnp.float32)


def core_half(value, axis, core, chips=PLANE):
    shape = value.shape
    split = shape[:axis] + (chips, 2, shape[axis] // (2 * chips)) + shape[axis + 1 :]
    half = pick(value.reshape(split), core, axis + 1)
    return half.reshape(shape[:axis] + (shape[axis] // 2,) + shape[axis + 1 :])


def core_merge(own, other, axis, core):
    shape = own.shape
    split = shape[:axis] + (PLANE, 1, shape[axis] // PLANE) + shape[axis + 1 :]
    own, other = (own.reshape(split), other.reshape(split))
    first = jnp.where(core == 0, own, other)
    second = jnp.where(core == 0, other, own)
    merged = jnp.concatenate([first, second], axis=axis + 1)
    return merged.reshape(shape[:axis] + (2 * shape[axis],) + shape[axis + 1 :])


def paired_device(
    latents,
    clip_text,
    embedding,
    lengths,
    conv_weight,
    up_weight,
    down_weight,
    hidden_vecs,
    vectors,
    time_weight,
    map_weight,
    attn_in,
    out_weight,
    grad_out,
):
    lat_count, band_rows, columns, channels = latents.shape
    height = band_rows * LINE
    pixels = height * columns
    text_len, clip_width = clip_text.shape[1:]
    hidden_width = up_weight.shape[1]
    time_rank = time_weight.shape[0]
    share = up_weight.shape[0]
    half_channels, half_hidden = (channels // 2, hidden_width // 2)
    head_count = half_channels // HEAD_DIM
    dp_index = lax.axis_index("dp")
    place = lax.axis_index("band")
    plane, core = (dp_index // 2, dp_index % 2)
    f32, low = (jnp.float32, jnp.bfloat16)

    latent = spread_line(latents, place).reshape(height, columns, channels)
    small_cols = jnp.concatenate([conv_weight, vectors], axis=0)
    small_all = gather_small(small_cols, plane, core, place)
    small_all = small_all.reshape((-1,) + small_cols.shape).transpose(1, 0, 2)
    small_all = small_all.reshape(small_cols.shape[0], channels).astype(f32)
    taps, vecs = (small_all[:9], small_all[9:])
    hidden_all = gather_small_line(hidden_vecs, plane, place)
    hidden_all = hidden_all.reshape((-1,) + hidden_vecs.shape).transpose(1, 0, 2)
    hidden_all = hidden_all.reshape(3, half_hidden).astype(f32)
    time_all = gather_small(time_weight, plane, core, place)
    time_all = time_all.reshape((-1,) + time_weight.shape).transpose(1, 0, 2)
    time_all = time_all.reshape(time_rank, 2 * channels)

    def with_partner(value, axis):
        kept = core_half(value, axis, core)
        got = swap(core_half(value, axis, 1 - core), 1)
        both = jnp.zeros((2,) + kept.shape, kept.dtype)
        return put(put(both, kept, core), got, 1 - core)

    up_shard = with_partner(up_weight, 1)
    attn_shard = with_partner(attn_in, 2).transpose(0, 2, 1, 3)
    attn_shard = attn_shard.reshape(2, share, 3 * half_channels)
    up_full, down_full, attn_full, map_full, out_full = gather_all(
        (up_shard, down_weight[None], attn_shard, map_weight[None], out_weight[None]),
        plane,
        place,
    )

    clip_own = pick(clip_text, place).astype(f32)
    words = pair(jax.nn.silu(clip_own).astype(low)).reshape(2 * text_len, clip_width)
    words_half = core_half(words, 1, core)
    lengths_two = pair(pick(lengths, place))
    embed_own = pick(embedding, place)

    framed = jnp.pad(latent, ((1, 1), (1, 1), (0, 0)))
    conv_out = jnp.broadcast_to(vecs[0], latent.shape)
    for offset in range(9):
        row_shift, col_shift = (offset // 3, offset % 3)
        conv_out = conv_out + taps[offset] * framed[
            row_shift : row_shift + height, col_shift : col_shift + columns
        ].astype(f32)
    first_norm, first_inv = norm_parts(conv_out.reshape(pixels, channels))
    first_in = pair(first_norm.astype(low)).reshape(2 * pixels, channels)
    up_out = product(first_in, up_full) + hidden_all[0]
    active = gelu_exact(up_out)
    active_lat = active.reshape(2, pixels, half_hidden)
    strength = jnp.sqrt(jnp.sum(active_lat * active_lat, axis=1))
    strength_sum = pair_sum(jnp.sum(strength, axis=-1, keepdims=True))
    grn_denom = strength_sum / hidden_width + 1e-06
    grn_ratio = strength / grn_denom
    gamma_vec = hidden_all[1]
    grn_out = (
        gamma_vec * (active_lat * grn_ratio[:, None]) + hidden_all[2] + active_lat
    ).astype(low)
    lowered = own_sum(product(grn_out[0], down_full), product(grn_out[1], down_full))
    first_sum = latent.reshape(pixels, channels).astype(f32) + (lowered + vecs[1])
    modulation = product(embed_own[None], time_all)[0]
    scale_vec = modulation[:channels] + vecs[2]
    shift_vec = modulation[channels:] + vecs[3]
    second = first_sum * (1.0 + scale_vec) + shift_vec
    second_norm, second_inv = norm_parts(second)
    second_in = pair(second_norm.astype(low)).reshape(2 * pixels, channels)

    mapped = pair_sum(product(words_half, map_full).reshape(2, text_len, channels))
    mapped = (mapped + vecs[4]).astype(low).reshape(2 * text_len, channels)
    bias = jnp.concatenate(
        [
            core_half(vecs[5], 0, core),
            jnp.zeros((half_channels,), f32),
            core_half(vecs[6], 0, core),
        ]
    )
    pixel_qkv = (product(second_in, attn_full) + bias).astype(low)
    text_kv = (
        product(mapped, attn_full[:, half_channels:]) + bias[half_channels:]
    ).astype(low)
    pixel_qkv = pixel_qkv.reshape(2, pixels, 3, head_count, HEAD_DIM)
    text_kv = text_kv.reshape(2, text_len, 2, head_count, HEAD_DIM)
    query = pixel_qkv[:, :, 0]
    key_rows = jnp.concatenate([pixel_qkv[:, :, 1], text_kv[:, :, 0]], axis=1)
    value_rows = jnp.concatenate([pixel_qkv[:, :, 2], text_kv[:, :, 1]], axis=1)
    key_places = jnp.arange(pixels + text_len, dtype=jnp.int32)
    valid_keys = key_places[None] < pixels + lengths_two[:, None]
    mixed, log_totals = lax.map(attend_one, (query, key_rows, value_rows, valid_keys))
    mixed = mixed.reshape(2, pixels, half_channels)
    attended = own_sum(product(mixed[0], out_full), product(mixed[1], out_full))
    layer_own = (second + (attended + vecs[7])).astype(low)
    layer_out = spread_line(layer_own.reshape(latents.shape), place)

    grad_own = spread_line(grad_out, place).reshape(pixels, channels)
    grad_two = pair(grad_own)
    g_mixed = product_nt(grad_two.reshape(2 * pixels, channels), out_full).astype(low)
    g_mixed = g_mixed.reshape(2, pixels, head_count, HEAD_DIM)

    def owner_sums(left, right, parts):
        block = left.shape[1] // PLANE
        half = right.shape[1] // 2

        def piece(chip, which):
            cut = lax.dynamic_slice_in_dim(left, chip * block, block, 1)
            return product_tn(cut, right[:, which * half : (which + 1) * half])

        return reduce_owner(piece, parts, plane, place)

    out_grad = owner_sums(
        mixed.reshape(2 * pixels, half_channels), grad_two.reshape(2 * pixels, channels), 1
    )[0]
    g_query, g_key, g_value = lax.map(
        attend_back, (query, key_rows, value_rows, valid_keys, log_totals, g_mixed)
    )
    g_key, g_value = (g_key.astype(low), g_value.astype(low))
    g_pixel = jnp.stack([g_query, g_key[:, :pixels], g_value[:, :pixels]], axis=2)
    g_pixel = g_pixel.reshape(2, pixels, 3 * half_channels)
    g_text = jnp.stack([g_key[:, pixels:], g_value[:, pixels:]], axis=2)
    g_text = g_text.reshape(2 * text_len, 2 * half_channels)
    g_second_in = own_sum(product_nt(g_pixel[0], attn_full), product_nt(g_pixel[1], attn_full))
    g_mapped = pair_sum(
        product_nt(g_text, attn_full[:, half_channels:]).reshape(2, text_len, channels)
    )
    g_mapped = g_mapped.astype(low).reshape(2 * text_len, channels)
    padded_text = jnp.concatenate([jnp.zeros((2 * text_len, half_channels), low), g_text], axis=1)
    attn_grad = owner_sums(
        jnp.concatenate([second_in, mapped], axis=0),
        jnp.concatenate([g_pixel.reshape(2 * pixels, 3 * half_channels), padded_text], axis=0),
        2,
    )
    map_grad = owner_sums(words_half, g_mapped, 1)[0]
    g_words = product_nt(g_mapped, map_full).reshape(2, text_len, clip_width // 2)
    g_words = core_merge(g_words[0], swap(g_words[1], 1), 1, core)
    sigmoid_text = jax.nn.sigmoid(clip_own)
    text_own = (g_words * (sigmoid_text * (1.0 + clip_own * (1.0 - sigmoid_text)))).astype(low)
    text_own = text_own.reshape(text_len, LINE, clip_width // LINE).transpose(1, 0, 2)
    text_grad = spread_line(text_own, place)

    grad_float = grad_own.astype(f32)
    g_second = grad_float + norm_back(g_second_in, second_norm, second_inv)
    g_scale = jnp.sum(g_second * first_sum, axis=0)
    g_shift = jnp.sum(g_second, axis=0)
    g_modulation = jnp.concatenate([g_scale, g_shift])
    time_part = embed_own.astype(f32)[:, None] * g_modulation[None]
    g_first = g_second * (1.0 + scale_vec)
    g_down_own = g_first.astype(low)
    g_down = pair(g_down_own).reshape(2 * pixels, channels)
    down_grad = owner_sums(grn_out.reshape(2 * pixels, half_hidden), g_down, 1)[0]
    g_grn = product_nt(g_down, down_full).reshape(2, pixels, half_hidden)
    g_grn_active = jnp.sum(g_grn * active_lat, axis=1)
    grad_gamma = jnp.sum(g_grn_active * grn_ratio, axis=0)
    grad_beta = jnp.sum(g_grn, axis=(0, 1))
    g_ratio = g_grn_active * gamma_vec
    ratio_sum = pair_sum(jnp.sum(g_ratio * strength, axis=-1, keepdims=True))
    g_strength = g_ratio / grn_denom - ratio_sum / (hidden_width * grn_denom * grn_denom)
    g_active = (
        g_grn * (1.0 + gamma_vec * grn_ratio[:, None])
        + active_lat * (g_strength / strength)[:, None]
    )
    gelu_value, gelu_pull = jax.vjp(gelu_exact, up_out)
    g_up = gelu_pull(g_active.reshape(2 * pixels, half_hidden))[0].astype(low)
    g_first_in = own_sum(
        product_nt(g_up[:pixels], up_full), product_nt(g_up[pixels:], up_full)
    )
    g_conv = norm_back(g_first_in, first_norm, first_inv).astype(low).reshape(latent.shape)
    up_grad = owner_sums(first_in, g_up, 2)
    g_framed = jnp.pad(g_conv, ((1, 1), (1, 1), (0, 0)))
    g_conv_f = g_conv.astype(f32)
    back_sum = g_first.reshape(latent.shape)
    tap_grads = []
    for offset in range(9):
        row_shift, col_shift = (offset // 3, offset % 3)
        window = framed[
            row_shift : row_shift + height, col_shift : col_shift + columns
        ].astype(f32)
        tap_grads.append(jnp.sum(g_conv_f * window, axis=(0, 1)))
        back_sum = back_sum + taps[offset] * g_framed[
            2 - row_shift : 2 - row_shift + height, 2 - col_shift : 2 - col_shift + columns
        ].astype(f32)
    latent_grad = spread_line(back_sum.astype(low).reshape(latents.shape), place)

    up_grad = core_merge(
        pick(up_grad, core), swap(pick(up_grad, 1 - core), 1), 1, core
    )
    attn_grad = attn_grad.reshape(2, share, 3, half_channels)
    attn_grad = core_merge(
        pick(attn_grad, core), swap(pick(attn_grad, 1 - core), 1), 2, core
    ).transpose(1, 0, 2)

    own_zero = jnp.zeros((half_channels,), f32)
    vec_parts = jnp.stack(
        [
            jnp.sum(g_conv_f, axis=(0, 1)),
            column_sums(g_down_own),
            g_scale,
            g_shift,
            column_sums(g_mapped[:text_len]),
            core_merge(column_sums(g_pixel.reshape(2 * pixels, -1)[:, :half_channels]), own_zero, 0, core),
            core_merge(
                column_sums(g_pixel.reshape(2 * pixels, -1)[:, 2 * half_channels :])
                + column_sums(g_text[:, half_channels:]),
                own_zero,
                0,
                core,
            ),
            jnp.sum(grad_float, axis=0),
        ]
    )
    col_parts = jnp.concatenate([jnp.stack(tap_grads), vec_parts])
    col_parts = col_parts.reshape(col_parts.shape[0], PLANE, 2, LINE, -1).transpose(1, 2, 3, 0, 4)
    col_parts = col_parts.reshape(PLANE, 2, LINE, -1)
    time_part = time_part.reshape(time_rank, PLANE, 2, LINE, -1).transpose(1, 2, 3, 0, 4)
    time_part = time_part.reshape(PLANE, 2, LINE, -1)
    core_parts = jnp.concatenate([col_parts, time_part], axis=-1)
    core_sum = pick(core_parts, core, 1) + swap(pick(core_parts, 1 - core, 1), 1)
    hidden_parts = jnp.stack([column_sums(g_up), grad_gamma, grad_beta])
    hidden_parts = hidden_parts.reshape(3, PLANE, LINE, -1).transpose(1, 2, 0, 3)
    hidden_parts = hidden_parts.reshape(PLANE, LINE, -1)
    small_sum = reduce_small(
        jnp.concatenate([core_sum, hidden_parts], axis=-1), plane, place
    )
    col_size, time_size = (17 * (channels // 32), time_rank * (channels // 16))
    col_grads = small_sum[:col_size].reshape(17, -1)
    time_grad = small_sum[col_size : col_size + time_size].reshape(time_rank, -1)
    hidden_grad = small_sum[col_size + time_size :].reshape(3, -1)
    return (
        layer_out,
        latent_grad,
        text_grad,
        col_grads[:9],
        up_grad,
        down_grad,
        hidden_grad,
        col_grads[9:],
        time_grad,
        map_grad,
        attn_grad,
        out_grad,
    )


def choose(latents, *rest):
    shape = {axis: lax.axis_size(axis) for axis in ("dp", "band")}
    fits = (
        shape["dp"] == 2 * PLANE
        and shape["band"] == LINE
        and latents.shape[0] == LINE
        and latents.shape[3] % (2 * PLANE * HEAD_DIM) == 0
    )
    return (paired_device if fits else per_device)(latents, *rest)


def solution(mesh):
    placed = (
        P("dp", "band", None, None),
        P("dp", None, None),
        P("dp", None),
        P("dp"),
        P(None, ("dp", "band")),
        P(("dp", "band"), None),
        P(("dp", "band"), None),
        P(None, ("dp", "band")),
        P(None, ("dp", "band")),
        P(None, ("dp", "band")),
        P(("dp", "band"), None),
        P(None, ("dp", "band"), None),
        P(("dp", "band"), None),
        P("dp", "band", None, None),
    )
    return jax.shard_map(
        choose,
        mesh=mesh,
        in_specs=placed,
        out_specs=(
            P("dp", "band", None, None),
            P("dp", "band", None, None),
            P("dp", None, "band"),
            P(None, ("dp", "band")),
            P(("dp", "band"), None),
            P(("dp", "band"), None),
            P(None, ("dp", "band")),
            P(None, ("dp", "band")),
            P(None, ("dp", "band")),
            P(("dp", "band"), None),
            P(None, ("dp", "band"), None),
            P(("dp", "band"), None),
        ),
        check_vma=False,
    )
```

```python
import functools

import jax
import jax.numpy as jnp
from jax import lax
from jax.experimental import pallas as pl
from jax.experimental.pallas import tpu as pltpu
from jax.sharding import PartitionSpec as P

HEAD_DIM = 64


def with_halo(array, sides, width):
    for axis, dim in sides:
        size, length = (lax.axis_size(axis), array.shape[dim])
        up = [(i, (i + 1) % size) for i in range(size - 1)]
        down = [(j, i) for i, j in up]
        last = lax.slice_in_dim(array, length - width, length, axis=dim)
        first = lax.slice_in_dim(array, 0, width, axis=dim)
        before = lax.ppermute(last, axis, up)
        after = lax.ppermute(first, axis, down)
        array = jnp.concatenate([before, array, after], axis=dim)
    return array


def product(left_op, right_op):
    return jnp.dot(left_op, right_op, preferred_element_type=jnp.float32)


def product_tn(left_op, right_op):
    return lax.dot_general(
        left_op, right_op, (((0,), (0,)), ((), ())), preferred_element_type=jnp.float32
    )


def product_nt(left_op, right_op):
    return lax.dot_general(
        left_op, right_op, (((1,), (1,)), ((), ())), preferred_element_type=jnp.float32
    )


def norm_parts(array_in):
    center = array_in - jnp.mean(array_in, axis=-1, keepdims=True)
    spread = jnp.mean(center * center, axis=-1, keepdims=True)
    inverse = lax.rsqrt(spread + 1e-06)
    return (center * inverse, inverse)


def norm_back(incoming, normed, inverse):
    return inverse * (
        incoming
        - jnp.mean(incoming, axis=-1, keepdims=True)
        - normed * jnp.mean(incoming * normed, axis=-1, keepdims=True)
    )


def column_sums(array_in):
    return jnp.sum(array_in.astype(jnp.float32), axis=0)


def gelu_exact(array_in):
    return jax.nn.gelu(array_in, approximate=False)


def masked_scores(query_one, key_one, valid_one):
    raw_scores = jnp.einsum(
        "qhd,khd->hqk", query_one, key_one, preferred_element_type=jnp.float32
    ) * HEAD_DIM ** (-0.5)
    return jnp.where(valid_one[None, None, :], raw_scores, -1000000000.0)


def attend_one(items):
    query_one, key_one, value_one, valid_one = items
    scores = masked_scores(query_one, key_one, valid_one)
    top_score = jnp.max(scores, axis=-1, keepdims=True)
    exponent = jnp.exp(scores - top_score)
    row_total = jnp.sum(exponent, axis=-1, keepdims=True)
    log_total = top_score + jnp.log(row_total)
    probs_low = (exponent / row_total).astype(jnp.bfloat16)
    mixed_one = jnp.einsum(
        "hqk,khd->qhd", probs_low, value_one, preferred_element_type=jnp.float32
    ).astype(jnp.bfloat16)
    return (mixed_one, log_total)


def attend_back(items):
    query_one, key_one, value_one, valid_one, log_one, gmix_one = items
    weights_again = jnp.exp(masked_scores(query_one, key_one, valid_one) - log_one)
    g_probs = jnp.einsum("qhd,khd->hqk", gmix_one, value_one, preferred_element_type=jnp.float32)
    inner_sum = jnp.sum(weights_again * g_probs, axis=-1, keepdims=True)
    g_score = (weights_again * (g_probs - inner_sum)).astype(jnp.bfloat16)
    probs_again = weights_again.astype(jnp.bfloat16)
    g_query = (
        jnp.einsum("hqk,khd->qhd", g_score, key_one, preferred_element_type=jnp.float32)
        * HEAD_DIM ** (-0.5)
    ).astype(jnp.bfloat16)
    g_key = jnp.einsum(
        "hqk,qhd->khd", g_score, query_one, preferred_element_type=jnp.float32
    ) * HEAD_DIM ** (-0.5)
    g_value = jnp.einsum("hqk,qhd->khd", probs_again, gmix_one, preferred_element_type=jnp.float32)
    return (g_query, g_key, g_value)


def per_device(
    latents,
    clip_text,
    embedding,
    lengths,
    conv_weight,
    up_weight,
    down_weight,
    hidden_vecs,
    vectors,
    time_weight,
    map_weight,
    attn_in,
    out_weight,
    grad_out,
):
    lat_count, band_rows, columns, channels = latents.shape
    tokens_lat = band_rows * columns
    tok_rows = lat_count * tokens_lat
    hidden_width = up_weight.shape[1]
    text_len = clip_text.shape[1]
    clip_width = clip_text.shape[2]
    band_size = lax.axis_size("band")
    band_index = lax.axis_index("band")
    pixel_count = tokens_lat * band_size
    head_count = channels // HEAD_DIM
    band_share = 1.0 / band_size
    res_shards = (conv_weight, up_weight, down_weight, hidden_vecs, vectors)
    attn_shards = (time_weight, map_weight, attn_in, out_weight)
    res_full = (
        lax.all_gather(res_shards[0], ("dp", "band"), axis=1, tiled=True),
        lax.all_gather(res_shards[1], ("dp", "band"), axis=0, tiled=True),
        lax.all_gather(res_shards[2], ("dp", "band"), axis=0, tiled=True),
        lax.all_gather(res_shards[3], ("dp", "band"), axis=1, tiled=True),
        lax.all_gather(res_shards[4], ("dp", "band"), axis=1, tiled=True),
    )
    attn_full = (
        lax.all_gather(attn_shards[0], ("dp", "band"), axis=1, tiled=True),
        lax.all_gather(attn_shards[1], ("dp", "band"), axis=0, tiled=True),
        lax.all_gather(attn_shards[2], ("dp", "band"), axis=1, tiled=True),
        lax.all_gather(attn_shards[3], ("dp", "band"), axis=0, tiled=True),
    )
    hidden_values = res_full[3].astype(jnp.float32)
    vec_values = res_full[4].astype(jnp.float32)
    framed = with_halo(latents, (("band", 1),), 1)
    framed = jnp.pad(framed, ((0, 0), (0, 0), (1, 1), (0, 0)))
    conv_taps = res_full[0].astype(jnp.float32)
    conv_out = jnp.broadcast_to(vec_values[0], latents.shape)
    for offset in range(9):
        row_shift = offset // 3
        col_shift = offset % 3
        conv_out = conv_out + conv_taps[offset] * framed[
            :, row_shift : row_shift + band_rows, col_shift : col_shift + columns
        ].astype(jnp.float32)
    first_norm, first_inv = norm_parts(conv_out.reshape(tok_rows, channels))
    first_in = first_norm.astype(jnp.bfloat16)
    up_out = product(first_in, res_full[1]) + hidden_values[0]
    active = gelu_exact(up_out)
    active_lat = active.reshape(lat_count, tokens_lat, hidden_width)
    square_sums = lax.psum(
        jnp.sum(active_lat * active_lat, axis=1).astype(jnp.bfloat16), "band"
    ).astype(jnp.float32)
    strength = jnp.sqrt(square_sums)
    grn_denom = jnp.mean(strength, axis=-1, keepdims=True) + 1e-06
    grn_ratio = strength / grn_denom
    gamma_vec = hidden_values[1]
    grn_out = (
        (gamma_vec * (active_lat * grn_ratio[:, None]) + hidden_values[2] + active_lat)
        .astype(jnp.bfloat16)
        .reshape(tok_rows, hidden_width)
    )
    first_sum = latents.reshape(tok_rows, channels).astype(jnp.float32) + (
        product(grn_out, res_full[2]) + vec_values[1]
    )
    modulation = product(embedding, attn_full[0])
    scale_vec = modulation[:, :channels] + vec_values[2]
    shift_vec = modulation[:, channels:] + vec_values[3]
    first_lat = first_sum.reshape(lat_count, tokens_lat, channels)
    second = first_lat * (1.0 + scale_vec[:, None]) + shift_vec[:, None]
    second_norm, second_inv = norm_parts(second)
    second_in = second_norm.astype(jnp.bfloat16).reshape(tok_rows, channels)
    clip_words = (
        jax.nn.silu(clip_text.astype(jnp.float32))
        .astype(jnp.bfloat16)
        .reshape(lat_count * text_len, clip_width)
    )
    mapped = (product(clip_words, attn_full[1]) + vec_values[4]).astype(jnp.bfloat16)
    projections = attn_full[2]
    query_rows = (product(second_in, projections[0]) + vec_values[5]).astype(jnp.bfloat16)
    pixel_key = (
        product(second_in, projections[1])
        .astype(jnp.bfloat16)
        .reshape(lat_count, tokens_lat, channels)
    )
    pixel_value = (
        (product(second_in, projections[2]) + vec_values[6])
        .astype(jnp.bfloat16)
        .reshape(lat_count, tokens_lat, channels)
    )
    all_key, all_value = (
        lax.all_gather(pixel_key, "band", axis=1, tiled=True),
        lax.all_gather(pixel_value, "band", axis=1, tiled=True),
    )
    text_key = (
        product(mapped, projections[1]).astype(jnp.bfloat16).reshape(lat_count, text_len, channels)
    )
    text_value = (
        (product(mapped, projections[2]) + vec_values[6])
        .astype(jnp.bfloat16)
        .reshape(lat_count, text_len, channels)
    )
    key_rows = jnp.concatenate([all_key, text_key], axis=1).reshape(
        lat_count, pixel_count + text_len, head_count, HEAD_DIM
    )
    value_rows = jnp.concatenate([all_value, text_value], axis=1).reshape(
        lat_count, pixel_count + text_len, head_count, HEAD_DIM
    )
    query_heads = query_rows.reshape(lat_count, tokens_lat, head_count, HEAD_DIM)
    key_places = jnp.arange(pixel_count + text_len, dtype=jnp.int32)
    valid_keys = key_places[None, :] < pixel_count + lengths[:, None]
    mixed_heads, log_totals = lax.map(attend_one, (query_heads, key_rows, value_rows, valid_keys))
    mixed_out = mixed_heads.reshape(tok_rows, channels)
    attended = product(mixed_out, attn_full[3]) + vec_values[7]
    layer_out = (
        (second.reshape(tok_rows, channels) + attended).astype(jnp.bfloat16).reshape(latents.shape)
    )
    res_back = (
        lax.all_gather(res_shards[0], ("dp", "band"), axis=1, tiled=True),
        lax.all_gather(res_shards[1], ("dp", "band"), axis=0, tiled=True),
        lax.all_gather(res_shards[2], ("dp", "band"), axis=0, tiled=True),
        lax.all_gather(res_shards[3], ("dp", "band"), axis=1, tiled=True),
        lax.all_gather(res_shards[4], ("dp", "band"), axis=1, tiled=True),
    )
    attn_back = (
        lax.all_gather(attn_shards[0], ("dp", "band"), axis=1, tiled=True),
        lax.all_gather(attn_shards[1], ("dp", "band"), axis=0, tiled=True),
        lax.all_gather(attn_shards[2], ("dp", "band"), axis=1, tiled=True),
        lax.all_gather(attn_shards[3], ("dp", "band"), axis=0, tiled=True),
    )
    proj_back = attn_back[2]
    grad_rows = grad_out.reshape(tok_rows, channels)
    grad_float = grad_rows.astype(jnp.float32)
    out_grad_w = product_tn(mixed_out, grad_rows)
    g_mixed = (
        product_nt(grad_rows, attn_back[3])
        .astype(jnp.bfloat16)
        .reshape(lat_count, tokens_lat, head_count, HEAD_DIM)
    )
    g_query_heads, g_key, g_value = lax.map(
        attend_back, (query_heads, key_rows, value_rows, valid_keys, log_totals, g_mixed)
    )
    g_query = g_query_heads.reshape(tok_rows, channels)
    g_key = g_key.reshape(lat_count, pixel_count + text_len, channels)
    g_value = g_value.reshape(lat_count, pixel_count + text_len, channels)
    pixel_gkey, pixel_gvalue = (
        lax.psum_scatter(
            g_key[:, :pixel_count].astype(jnp.bfloat16), "band", scatter_dimension=1, tiled=True
        ).astype(jnp.float32),
        lax.psum_scatter(
            g_value[:, :pixel_count].astype(jnp.bfloat16), "band", scatter_dimension=1, tiled=True
        ).astype(jnp.float32),
    )
    text_gkey, text_gvalue = (
        lax.psum(g_key[:, pixel_count:].astype(jnp.bfloat16), "band").astype(jnp.float32),
        lax.psum(g_value[:, pixel_count:].astype(jnp.bfloat16), "band").astype(jnp.float32),
    )
    pixel_kb = pixel_gkey.astype(jnp.bfloat16).reshape(tok_rows, channels)
    pixel_vb = pixel_gvalue.astype(jnp.bfloat16).reshape(tok_rows, channels)
    text_kb = text_gkey.astype(jnp.bfloat16).reshape(lat_count * text_len, channels)
    text_vb = text_gvalue.astype(jnp.bfloat16).reshape(lat_count * text_len, channels)
    g_second_in = (
        product_nt(g_query, proj_back[0])
        + product_nt(pixel_kb, proj_back[1])
        + product_nt(pixel_vb, proj_back[2])
    )
    grad_query_w = product_tn(second_in, g_query)
    grad_key_w = product_tn(second_in, pixel_kb) + band_share * product_tn(mapped, text_kb)
    grad_value_w = product_tn(second_in, pixel_vb) + band_share * product_tn(mapped, text_vb)
    g_mapped = (product_nt(text_kb, proj_back[1]) + product_nt(text_vb, proj_back[2])).astype(
        jnp.bfloat16
    )
    grad_map_w = band_share * product_tn(clip_words, g_mapped)
    clip_slice = clip_width // band_size
    map_rows = lax.dynamic_slice_in_dim(attn_back[1], band_index * clip_slice, clip_slice, 0)
    text_part = lax.dynamic_slice_in_dim(clip_text, band_index * clip_slice, clip_slice, 2).astype(
        jnp.float32
    )
    sigmoid_text = jax.nn.sigmoid(text_part)
    g_words = product_nt(g_mapped, map_rows).reshape(lat_count, text_len, clip_slice)
    text_grad = (g_words * (sigmoid_text * (1.0 + text_part * (1.0 - sigmoid_text)))).astype(
        jnp.bfloat16
    )
    g_second = grad_float.reshape(lat_count, tokens_lat, channels) + norm_back(
        g_second_in.reshape(lat_count, tokens_lat, channels), second_norm, second_inv
    )
    g_scale = jnp.sum(g_second * first_lat, axis=1)
    g_shift = jnp.sum(g_second, axis=1)
    grad_time_w = lax.dot_general(
        embedding.astype(jnp.float32),
        jnp.concatenate([g_scale, g_shift], axis=1),
        (((0,), (0,)), ((), ())),
        precision=lax.Precision.HIGHEST,
        preferred_element_type=jnp.float32,
    )
    attn_grads = (
        lax.psum_scatter(grad_time_w, ("dp", "band"), scatter_dimension=1, tiled=True),
        lax.psum_scatter(grad_map_w, ("dp", "band"), scatter_dimension=0, tiled=True),
        lax.psum_scatter(
            jnp.stack([grad_query_w, grad_key_w, grad_value_w]),
            ("dp", "band"),
            scatter_dimension=1,
            tiled=True,
        ),
        lax.psum_scatter(out_grad_w, ("dp", "band"), scatter_dimension=0, tiled=True),
    )
    g_first = g_second * (1.0 + scale_vec[:, None])
    g_down = g_first.astype(jnp.bfloat16).reshape(tok_rows, channels)
    grad_down_w = product_tn(grn_out, g_down)
    g_grn = product_nt(g_down, res_back[2]).reshape(lat_count, tokens_lat, hidden_width)
    grad_gamma = jnp.sum(g_grn * active_lat * grn_ratio[:, None], axis=(0, 1))
    grad_beta = jnp.sum(g_grn, axis=(0, 1))
    g_ratio = lax.psum(
        jnp.sum(g_grn * gamma_vec * active_lat, axis=1).astype(jnp.bfloat16), "band"
    ).astype(jnp.float32)
    g_strength = g_ratio / grn_denom - jnp.sum(g_ratio * strength, axis=-1, keepdims=True) / (
        hidden_width * grn_denom * grn_denom
    )
    g_active = (
        g_grn * (1.0 + gamma_vec * grn_ratio[:, None])
        + active_lat * (g_strength / strength)[:, None]
    )
    gelu_value, gelu_pull = jax.vjp(gelu_exact, up_out)
    g_up = gelu_pull(g_active.reshape(tok_rows, hidden_width))[0].astype(jnp.bfloat16)
    grad_up_w = product_tn(first_in, g_up)
    g_conv = (
        norm_back(product_nt(g_up, res_back[1]), first_norm, first_inv)
        .astype(jnp.bfloat16)
        .reshape(latents.shape)
    )
    g_framed = with_halo(g_conv, (("band", 1),), 1)
    g_framed = jnp.pad(g_framed, ((0, 0), (0, 0), (1, 1), (0, 0)))
    conv_back = res_back[0].astype(jnp.float32)
    g_conv_f = g_conv.astype(jnp.float32)
    back_sum = g_first.reshape(latents.shape)
    tap_grads = []
    for offset in range(9):
        row_shift = offset // 3
        col_shift = offset % 3
        window = framed[
            :, row_shift : row_shift + band_rows, col_shift : col_shift + columns
        ].astype(jnp.float32)
        tap_grads.append(jnp.sum(g_conv_f * window, axis=(0, 1, 2)))
        back_sum = back_sum + conv_back[offset] * g_framed[
            :, 2 - row_shift : 2 - row_shift + band_rows, 2 - col_shift : 2 - col_shift + columns
        ].astype(jnp.float32)
    latent_grad = back_sum.astype(jnp.bfloat16)
    grad_vectors = jnp.stack(
        [
            jnp.sum(g_conv_f, axis=(0, 1, 2)),
            column_sums(g_down),
            jnp.sum(g_scale, axis=0),
            jnp.sum(g_shift, axis=0),
            band_share * column_sums(g_mapped),
            column_sums(g_query),
            column_sums(pixel_vb) + band_share * column_sums(text_vb),
            jnp.sum(grad_float, axis=0),
        ]
    )
    grad_hidden = jnp.stack([column_sums(g_up), grad_gamma, grad_beta])
    grad_conv_w = jnp.stack(tap_grads)
    res_grads = (
        lax.psum_scatter(grad_conv_w, ("dp", "band"), scatter_dimension=1, tiled=True),
        lax.psum_scatter(grad_up_w, ("dp", "band"), scatter_dimension=0, tiled=True),
        lax.psum_scatter(grad_down_w, ("dp", "band"), scatter_dimension=0, tiled=True),
        lax.psum_scatter(grad_hidden, ("dp", "band"), scatter_dimension=1, tiled=True),
        lax.psum_scatter(grad_vectors, ("dp", "band"), scatter_dimension=1, tiled=True),
    )
    return (
        layer_out,
        latent_grad,
        text_grad,
        res_grads[0],
        res_grads[1],
        res_grads[2],
        res_grads[3],
        res_grads[4],
        attn_grads[0],
        attn_grads[1],
        attn_grads[2],
        attn_grads[3],
    )


PLANE = 4
LINE = 4
PAIR = 2 * HEAD_DIM


def key_bias(length, keys, pixels):
    rows = lax.broadcasted_iota(jnp.int32, (keys, 1), 0)
    return jnp.where(rows < pixels + length, 0.0, -1000000000.0)


def one_head(value, head):
    lanes = lax.broadcasted_iota(jnp.int32, value.shape, 1)
    return jnp.where((lanes // HEAD_DIM) == head, value, jnp.zeros_like(value))


def attend_kernel(pixels, length_ref, rows_ref, mixed_ref, log_ref):
    keys = rows_ref.shape[1]
    bias = key_bias(length_ref[pl.program_id(0)], keys, pixels)
    query = rows_ref[0, :pixels, :PAIR] * HEAD_DIM ** (-0.5)
    key = rows_ref[0, :, PAIR : 2 * PAIR]
    value = rows_ref[0, :, 2 * PAIR :]
    total = jnp.zeros((pixels, PAIR), jnp.float32)
    for head in range(PAIR // HEAD_DIM):
        scores = product_nt(key, one_head(query, head)) + bias
        top = jnp.max(scores, axis=0, keepdims=True)
        exponent = jnp.exp(scores - top)
        row_total = jnp.sum(exponent, axis=0, keepdims=True)
        probs = (exponent * (1.0 / row_total)).astype(jnp.bfloat16)
        total = total + product_tn(probs, one_head(value, head))
        log_ref[0, 0, head : head + 1, :] = top + jnp.log(row_total)
    mixed_ref[0] = total.astype(jnp.bfloat16)


def attend_back_kernel(pixels, length_ref, rows_ref, gmix_ref, log_ref, grad_ref):
    keys = rows_ref.shape[1]
    bias = key_bias(length_ref[pl.program_id(0)], keys, pixels)
    query = rows_ref[0, :pixels, :PAIR] * HEAD_DIM ** (-0.5)
    key = rows_ref[0, :, PAIR : 2 * PAIR]
    value = rows_ref[0, :, 2 * PAIR :]
    g_query = jnp.zeros((pixels, PAIR), jnp.float32)
    g_key = jnp.zeros((keys, PAIR), jnp.float32)
    g_value = jnp.zeros((keys, PAIR), jnp.float32)
    for head in range(PAIR // HEAD_DIM):
        query_one = one_head(query, head)
        gmix_one = one_head(gmix_ref[0], head)
        scores = product_nt(key, query_one) + bias
        weights = jnp.exp(scores - log_ref[0, 0, head : head + 1, :])
        g_probs = product_nt(value, gmix_one)
        inner = jnp.sum(weights * g_probs, axis=0, keepdims=True)
        g_score = (weights * (g_probs - inner)).astype(jnp.bfloat16)
        g_key = g_key + product(g_score, query_one)
        g_value = g_value + product(weights.astype(jnp.bfloat16), gmix_one)
        g_query = g_query + product_tn(g_score, one_head(key, head))
    g_query = (g_query * HEAD_DIM ** (-0.5)).astype(jnp.bfloat16)
    grad_ref[0, :pixels, :PAIR] = g_query
    grad_ref[0, pixels:, :PAIR] = jnp.zeros((keys - pixels, PAIR), jnp.bfloat16)
    grad_ref[0, :, PAIR : 2 * PAIR] = g_key.astype(jnp.bfloat16)
    grad_ref[0, :, 2 * PAIR :] = g_value.astype(jnp.bfloat16)


def attend_specs(keys, pixels):
    rows = pl.BlockSpec((1, keys, 3 * PAIR), lambda i, j, n: (i, 0, j))
    narrow = pl.BlockSpec((1, pixels, PAIR), lambda i, j, n: (i, 0, j))
    logs = pl.BlockSpec((1, 1, PAIR // HEAD_DIM, pixels), lambda i, j, n: (i, j, 0, 0))
    return (rows, narrow, logs)


def attend(rows, lengths, pixels):
    count, keys, width = rows.shape
    groups = width // (3 * PAIR)
    rows_spec, narrow, logs = attend_specs(keys, pixels)
    return pl.pallas_call(
        functools.partial(attend_kernel, pixels),
        out_shape=(
            jax.ShapeDtypeStruct((count, pixels, groups * PAIR), jnp.bfloat16),
            jax.ShapeDtypeStruct((count, groups, PAIR // HEAD_DIM, pixels), jnp.float32),
        ),
        grid_spec=pltpu.PrefetchScalarGridSpec(
            num_scalar_prefetch=1,
            grid=(count, groups),
            in_specs=[rows_spec],
            out_specs=[narrow, logs],
        ),
        compiler_params=pltpu.CompilerParams(vmem_limit_bytes=40 << 20),
        cost_estimate=pl.CostEstimate(
            flops=count * groups * 8 * pixels * keys * PAIR,
            bytes_accessed=rows.size * 3,
            transcendentals=2 * count * groups * pixels * keys,
        ),
        name="attend",
    )(lengths, rows)


def attend_back_pairs(rows, g_mixed, logs_in, lengths, pixels):
    count, keys, width = rows.shape
    groups = width // (3 * PAIR)
    rows_spec, narrow, logs = attend_specs(keys, pixels)
    return pl.pallas_call(
        functools.partial(attend_back_kernel, pixels),
        out_shape=jax.ShapeDtypeStruct(rows.shape, jnp.bfloat16),
        grid_spec=pltpu.PrefetchScalarGridSpec(
            num_scalar_prefetch=1,
            grid=(count, groups),
            in_specs=[rows_spec, narrow, logs],
            out_specs=rows_spec,
        ),
        compiler_params=pltpu.CompilerParams(vmem_limit_bytes=40 << 20),
        cost_estimate=pl.CostEstimate(
            flops=count * groups * 20 * pixels * keys * PAIR,
            bytes_accessed=rows.size * 5,
            transcendentals=2 * count * groups * pixels * keys,
        ),
        name="attend_back",
    )(lengths, rows, g_mixed, logs_in)


def swap(value, bit):
    return lax.ppermute(value, "dp", [(i, i ^ bit) for i in range(2 * PLANE)])


def rotate(value, step):
    return lax.ppermute(value, "band", [(i, (i + step) % LINE) for i in range(LINE)])


def pick(value, index, axis=0):
    return lax.dynamic_index_in_dim(value, index, axis, keepdims=False)


def put(buffer, value, index, axis=0):
    return lax.dynamic_update_index_in_dim(buffer, value, index, axis)


def spread_line(blocks, place):
    result = jnp.zeros(blocks.shape, blocks.dtype)
    result = put(result, pick(blocks, place), place)
    for step in range(1, LINE):
        moved = rotate(pick(blocks, (place + step) % LINE), step)
        result = put(result, moved, (place - step) % LINE)
    return result


def gather_line(shard, place):
    parts, rows, cols = shard.shape
    result = jnp.zeros((parts, LINE, rows, cols), shard.dtype)
    result = put(result, shard, place, 1)
    for step in range(1, LINE):
        result = put(result, rotate(shard, step), (place - step) % LINE, 1)
    return result


def gather_plane(block, plane):
    rows, cols = block.shape
    half = rows // 2
    by_x, by_y = (swap(block, 2), swap(block, 4))
    upper = swap(by_y[:half], 2)
    lower = swap(by_x[half:], 4)
    result = jnp.zeros((PLANE, rows, cols), block.dtype)
    result = put(result, block, plane)
    result = put(result, by_x, plane ^ 1)
    result = put(result, by_y, plane ^ 2)
    zero = jnp.int32(0)
    result = lax.dynamic_update_slice(result, upper[None], (plane ^ 3, zero, zero))
    result = lax.dynamic_update_slice(result, lower[None], (plane ^ 3, zero + half, zero))
    return (result, (by_x, by_y))


def held(*values):
    return lax.optimization_barrier(values)


def flat_line(shard, place):
    parts, rows, cols = shard.shape
    return gather_line(shard, place).reshape(parts * LINE * rows, cols)


def flat_plane(line, plane):
    full, _ = gather_plane(line, plane)
    return full.reshape(-1, line.shape[1])


def reduce_owner(piece, parts, plane, place):
    low = jnp.bfloat16
    far = [piece(plane ^ 3, half).astype(low) for half in range(2)]
    via_x, via_y = (swap(far[0], 2), swap(far[1], 4))
    out_x = [piece(plane ^ 1, 0).astype(low), None]
    out_y = [None, piece(plane ^ 2, 1).astype(low)]
    got_x, got_y = ([swap(out_x[0], 2), None], [None, swap(out_y[1], 4)])
    out_x[1] = (piece(plane ^ 1, 1) + via_y.astype(jnp.float32)).astype(low)
    out_y[0] = (piece(plane ^ 2, 0) + via_x.astype(jnp.float32)).astype(low)
    got_x[1], got_y[0] = (swap(out_x[1], 2), swap(out_y[0], 4))
    results = []
    for half in range(2):
        total = (
            piece(plane, half)
            + got_x[half].astype(jnp.float32)
            + got_y[half].astype(jnp.float32)
        )
        rows, cols = total.shape
        total = total.reshape(parts, LINE, rows // (parts * LINE), cols)
        summed = pick(total, place, 1)
        for step in range(1, LINE):
            sent = pick(total, (place + step) % LINE, 1).astype(low)
            summed = summed + rotate(sent, step).astype(jnp.float32)
        results.append(summed)
    return jnp.concatenate(results, axis=-1)


def gather_small(value, plane, core, place):
    cores = jnp.zeros((2,) + value.shape, value.dtype)
    cores = put(put(cores, value, core), swap(value, 1), 1 - core)
    full = gather_small_plane(cores, plane)
    line = jnp.zeros((LINE,) + full.shape, value.dtype)
    line = put(line, full, place)
    for step in range(1, LINE):
        line = put(line, rotate(full, step), (place - step) % LINE)
    return line


def gather_small_plane(line, plane):
    by_x = swap(line, 2)
    both = jnp.stack([line, by_x])
    by_y = swap(both, 4)
    full = jnp.zeros((PLANE,) + line.shape, line.dtype)
    full = put(put(full, line, plane), by_x, plane ^ 1)
    return put(put(full, by_y[0], plane ^ 2), by_y[1], plane ^ 3)


def reduce_small(value, plane, place):
    both = jnp.stack([pick(value, plane ^ 1), pick(value, plane ^ 3)])
    by_x = swap(both, 2)
    mine = pick(value, plane) + by_x[0]
    other = pick(value, plane ^ 2) + by_x[1]
    mine = mine + swap(other, 4)
    summed = pick(mine, place)
    for step in range(1, LINE):
        summed = summed + rotate(pick(mine, (place + step) % LINE), step)
    return summed


def pair(value):
    return jnp.stack([value, swap(value, 1)])


def pair_sum(value):
    return value + swap(value, 1)[::-1]


def own_sum(own, partner):
    return own + swap(partner.astype(jnp.bfloat16), 1).astype(jnp.float32)


def core_half(value, axis, core, chips=PLANE):
    shape = value.shape
    split = shape[:axis] + (chips, 2, shape[axis] // (2 * chips)) + shape[axis + 1 :]
    half = pick(value.reshape(split), core, axis + 1)
    return half.reshape(shape[:axis] + (shape[axis] // 2,) + shape[axis + 1 :])


def core_merge(own, other, axis, core):
    shape = own.shape
    split = shape[:axis] + (PLANE, 1, shape[axis] // PLANE) + shape[axis + 1 :]
    own, other = (own.reshape(split), other.reshape(split))
    first = jnp.where(core == 0, own, other)
    second = jnp.where(core == 0, other, own)
    merged = jnp.concatenate([first, second], axis=axis + 1)
    return merged.reshape(shape[:axis] + (2 * shape[axis],) + shape[axis + 1 :])


def paired_device(
    latents,
    clip_text,
    embedding,
    lengths,
    conv_weight,
    up_weight,
    down_weight,
    hidden_vecs,
    vectors,
    time_weight,
    map_weight,
    attn_in,
    out_weight,
    grad_out,
):
    lat_count, band_rows, columns, channels = latents.shape
    height = band_rows * LINE
    pixels = height * columns
    text_len, clip_width = clip_text.shape[1:]
    hidden_width = up_weight.shape[1]
    time_rank = time_weight.shape[0]
    half_channels, half_hidden = (channels // 2, hidden_width // 2)
    dp_index = lax.axis_index("dp")
    place = lax.axis_index("band")
    plane, core = (dp_index // 2, dp_index % 2)
    f32, low = (jnp.float32, jnp.bfloat16)

    small = jnp.concatenate(
        [conv_weight.reshape(-1), vectors.reshape(-1), hidden_vecs.reshape(-1)]
    )
    small_all = gather_small(small, plane, core, place).astype(f32)
    col_rows, col_width = (9 + vectors.shape[0], conv_weight.shape[1])
    col_all = small_all[..., : col_rows * col_width]
    col_all = col_all.reshape(LINE, PLANE, 2, col_rows, col_width).transpose(3, 1, 2, 0, 4)
    col_all = col_all.reshape(col_rows, channels)
    taps, vecs = (col_all[:9], col_all[9:])
    hidden_all = pick(small_all[..., col_rows * col_width :], core, 2)
    hidden_all = hidden_all.reshape(LINE, PLANE, 3, -1).transpose(2, 1, 0, 3)
    hidden_all = hidden_all.reshape(3, half_hidden)

    def with_partner(value, axis):
        kept = core_half(value, axis, core)
        got = swap(core_half(value, axis, 1 - core), 1)
        both = jnp.zeros((2,) + kept.shape, kept.dtype)
        return put(put(both, kept, core), got, 1 - core)

    def attn_order(value):
        groups = jnp.moveaxis(value.reshape(value.shape[:-1] + (-1, PAIR)), 0, -2)
        return groups.reshape(groups.shape[:-3] + (-1,))

    def attn_back_order(value):
        groups = jnp.moveaxis(value.reshape(value.shape[:-1] + (-1, 3, PAIR)), -2, 0)
        return groups.reshape(groups.shape[:-2] + (-1,))

    up_shard = with_partner(up_weight, 1)
    attn_shard = attn_order(jnp.moveaxis(with_partner(attn_in, 2), 1, 0))

    latent = spread_line(latents, place).reshape(height, columns, channels)
    up_line = flat_line(up_shard, place)
    up_line, latent, down_shard, map_shard, time_shard = held(
        up_line, latent, down_weight[None], map_weight[None], time_weight
    )
    up_full = flat_plane(up_line, plane)
    down_line = flat_line(down_shard, place)
    map_line = flat_line(map_shard, place)
    time_all = gather_small(time_shard, plane, core, place).transpose(3, 1, 2, 0, 4)
    time_all = time_all.reshape(time_rank, 2 * channels)
    clip_own = pick(clip_text, place).astype(f32)
    words_own = jax.nn.silu(clip_own).astype(low)
    text_pad = -(-text_len // 16) * 16
    words_own = jnp.pad(words_own, ((0, text_pad - text_len), (0, 0)))
    words = pair(words_own).reshape(2 * text_pad, clip_width)
    words_half = core_half(words, 1, core)
    lengths_two = pair(pick(lengths, place))
    embed_own = pick(embedding, place)

    framed = jnp.pad(latent, ((1, 1), (1, 1), (0, 0)))
    conv_out = jnp.broadcast_to(vecs[0], latent.shape)
    for offset in range(9):
        row_shift, col_shift = (offset // 3, offset % 3)
        conv_out = conv_out + taps[offset] * framed[
            row_shift : row_shift + height, col_shift : col_shift + columns
        ].astype(f32)
    first_norm, first_inv = norm_parts(conv_out.reshape(pixels, channels))
    first_in = pair(first_norm.astype(low)).reshape(2 * pixels, channels)
    up_full, down_line, map_line, first_in, words_half, attn_shard = held(
        up_full, down_line, map_line, first_in, words_half, attn_shard
    )
    down_full = flat_plane(down_line, plane)
    map_full = flat_plane(map_line, plane)
    attn_line = flat_line(attn_shard, place)
    up_out = product(first_in, up_full) + hidden_all[0]
    below = 0.5 + 0.5 * lax.erf(up_out * 0.5**0.5)
    slope = below + up_out * ((0.5 / jnp.pi) ** 0.5 * jnp.exp(-0.5 * up_out * up_out))
    active, slope = held((up_out * below).astype(low), slope.astype(low))
    active_lat = active.reshape(2, pixels, half_hidden).astype(f32)
    strength = jnp.sqrt(jnp.sum(active_lat * active_lat, axis=1))
    strength_sum = pair_sum(jnp.sum(strength, axis=-1, keepdims=True))
    grn_denom = strength_sum / hidden_width + 1e-06
    grn_ratio = strength / grn_denom
    gamma_vec = hidden_all[1]
    grn_out = (
        gamma_vec * (active_lat * grn_ratio[:, None]) + hidden_all[2] + active_lat
    ).astype(low)
    grn_out, down_full, map_full, attn_line, out_shard = held(
        grn_out, down_full, map_full, attn_line, out_weight[None]
    )
    attn_full = flat_plane(attn_line, plane)
    out_line = flat_line(out_shard, place)
    lowered = own_sum(product(grn_out[0], down_full), product(grn_out[1], down_full))
    first_sum = latent.reshape(pixels, channels).astype(f32) + (lowered + vecs[1])
    modulation = product(embed_own[None], time_all)[0]
    scale_vec = modulation[:channels] + vecs[2]
    shift_vec = modulation[channels:] + vecs[3]
    second = first_sum * (1.0 + scale_vec) + shift_vec
    second_norm, second_inv = norm_parts(second)
    mapped = pair_sum(product(words_half, map_full).reshape(2, text_pad, channels))
    mapped = (mapped + vecs[4]).astype(low)
    sources = jnp.concatenate([pair(second_norm.astype(low)), mapped], axis=1)
    keys = pixels + text_pad
    sources, attn_full, out_line, grad_shard = held(sources, attn_full, out_line, grad_out)
    sources = sources.reshape(2 * keys, channels)
    out_full = flat_plane(out_line, plane)
    grad_own = spread_line(grad_shard, place).reshape(pixels, channels)
    bias = jnp.stack([vecs[5], jnp.zeros((channels,), f32), vecs[6]])
    bias = attn_order(core_half(bias, 1, core))
    rows_qkv = (product(sources, attn_full) + bias).astype(low)
    rows_qkv = rows_qkv.reshape(2, keys, 3 * half_channels)
    mixed, log_totals = attend(rows_qkv, lengths_two, pixels)
    attended = own_sum(product(mixed[0], out_full), product(mixed[1], out_full))
    layer_own = (second + (attended + vecs[7])).astype(low)
    layer_out = spread_line(layer_own.reshape(latents.shape), place)

    grad_two = pair(grad_own)
    g_mixed = product_nt(grad_two.reshape(2 * pixels, channels), out_full).astype(low)
    g_mixed = g_mixed.reshape(2, pixels, half_channels)

    def owner_sums(left, right, parts):
        block = left.shape[1] // PLANE
        half = right.shape[1] // 2

        def piece(chip, which):
            cut = lax.dynamic_slice_in_dim(left, chip * block, block, 1)
            return product_tn(cut, right[:, which * half : (which + 1) * half])

        return reduce_owner(piece, parts, plane, place)

    out_grad = owner_sums(
        mixed.reshape(2 * pixels, half_channels), grad_two.reshape(2 * pixels, channels), 1
    )[0]
    g_rows = attend_back_pairs(rows_qkv, g_mixed, log_totals, lengths_two, pixels)
    g_second_in = own_sum(
        product_nt(g_rows[0, :pixels], attn_full), product_nt(g_rows[1, :pixels], attn_full)
    )
    g_text = g_rows[:, pixels:].reshape(2 * text_pad, 3 * half_channels)
    g_mapped = pair_sum(product_nt(g_text, attn_full).reshape(2, text_pad, channels))
    g_mapped = g_mapped.astype(low).reshape(2 * text_pad, channels)
    g_flat = g_rows.reshape(2 * keys, 3 * half_channels)
    attn_grad = owner_sums(sources, g_flat, 2)
    map_grad = owner_sums(words_half, g_mapped, 1)[0]
    g_words = product_nt(g_mapped, map_full).reshape(2, text_pad, -1)[:, :text_len]
    g_words = core_merge(g_words[0], swap(g_words[1], 1), 1, core)
    sigmoid_text = jax.nn.sigmoid(clip_own)
    text_own = (g_words * (sigmoid_text * (1.0 + clip_own * (1.0 - sigmoid_text)))).astype(low)
    text_own = text_own.reshape(text_len, LINE, clip_width // LINE).transpose(1, 0, 2)
    text_grad = spread_line(text_own, place)

    grad_float = grad_own.astype(f32)
    g_second = grad_float + norm_back(g_second_in, second_norm, second_inv)
    g_scale = jnp.sum(g_second * first_sum, axis=0)
    g_shift = jnp.sum(g_second, axis=0)
    g_modulation = jnp.concatenate([g_scale, g_shift])
    time_part = embed_own.astype(f32)[:, None] * g_modulation[None]
    g_first = g_second * (1.0 + scale_vec)
    g_down_own = g_first.astype(low)
    g_down = pair(g_down_own).reshape(2 * pixels, channels)
    down_grad = owner_sums(grn_out.reshape(2 * pixels, half_hidden), g_down, 1)[0]
    g_grn = product_nt(g_down, down_full).reshape(2, pixels, half_hidden)
    g_grn_active = jnp.sum(g_grn * active_lat, axis=1)
    g_grn_sum = jnp.sum(g_grn, axis=(0, 1))
    g_grn, g_grn_active, grad_beta = held(g_grn.astype(low), g_grn_active, g_grn_sum)
    g_grn = g_grn.astype(f32)
    grad_gamma = jnp.sum(g_grn_active * grn_ratio, axis=0)
    g_ratio = g_grn_active * gamma_vec
    ratio_sum = pair_sum(jnp.sum(g_ratio * strength, axis=-1, keepdims=True))
    g_strength = g_ratio / grn_denom - ratio_sum / (hidden_width * grn_denom * grn_denom)
    g_active = (
        g_grn * (1.0 + gamma_vec * grn_ratio[:, None])
        + active_lat * (g_strength / strength)[:, None]
    )
    g_up = (g_active.reshape(2 * pixels, half_hidden) * slope.astype(f32)).astype(low)
    g_first_in = own_sum(
        product_nt(g_up[:pixels], up_full), product_nt(g_up[pixels:], up_full)
    )
    g_conv = norm_back(g_first_in, first_norm, first_inv).astype(low).reshape(latent.shape)
    up_grad = owner_sums(first_in, g_up, 2)
    g_framed = jnp.pad(g_conv, ((1, 1), (1, 1), (0, 0)))
    g_conv_f = g_conv.astype(f32)
    back_sum = g_first.reshape(latent.shape)
    tap_grads = []
    for offset in range(9):
        row_shift, col_shift = (offset // 3, offset % 3)
        window = framed[
            row_shift : row_shift + height, col_shift : col_shift + columns
        ].astype(f32)
        tap_grads.append(jnp.sum(g_conv_f * window, axis=(0, 1)))
        back_sum = back_sum + taps[offset] * g_framed[
            2 - row_shift : 2 - row_shift + height, 2 - col_shift : 2 - col_shift + columns
        ].astype(f32)
    latent_grad = spread_line(back_sum.astype(low).reshape(latents.shape), place)

    up_grad = core_merge(
        pick(up_grad, core), swap(pick(up_grad, 1 - core), 1), 1, core
    )
    attn_grad = core_merge(
        attn_back_order(pick(attn_grad, core)),
        attn_back_order(swap(pick(attn_grad, 1 - core), 1)),
        2,
        core,
    )
    column_grads = attn_back_order(column_sums(g_flat))
    own_zero = jnp.zeros((half_channels,), f32)
    vec_parts = jnp.stack(
        [
            jnp.sum(g_conv_f, axis=(0, 1)),
            column_sums(g_down_own),
            g_scale,
            g_shift,
            column_sums(g_mapped[:text_pad]),
            core_merge(column_grads[0], own_zero, 0, core),
            core_merge(column_grads[2], own_zero, 0, core),
            jnp.sum(grad_float, axis=0),
        ]
    )
    col_parts = jnp.concatenate([jnp.stack(tap_grads), vec_parts])
    col_parts = col_parts.reshape(col_parts.shape[0], PLANE, 2, LINE, -1).transpose(1, 2, 3, 0, 4)
    col_parts = col_parts.reshape(PLANE, 2, LINE, -1)
    time_part = time_part.reshape(time_rank, PLANE, 2, LINE, -1).transpose(1, 2, 3, 0, 4)
    time_part = time_part.reshape(PLANE, 2, LINE, -1)
    core_parts = jnp.concatenate([col_parts, time_part], axis=-1)
    core_sum = pick(core_parts, core, 1) + swap(pick(core_parts, 1 - core, 1), 1)
    hidden_parts = jnp.stack([column_sums(g_up), grad_gamma, grad_beta])
    hidden_parts = hidden_parts.reshape(3, PLANE, LINE, -1).transpose(1, 2, 0, 3)
    hidden_parts = hidden_parts.reshape(PLANE, LINE, -1)
    small_sum = reduce_small(
        jnp.concatenate([core_sum, hidden_parts], axis=-1), plane, place
    )
    col_size, time_size = (17 * (channels // 32), time_rank * (channels // 16))
    col_grads = small_sum[:col_size].reshape(17, -1)
    time_grad = small_sum[col_size : col_size + time_size].reshape(time_rank, -1)
    hidden_grad = small_sum[col_size + time_size :].reshape(3, -1)
    return (
        layer_out,
        latent_grad,
        text_grad,
        col_grads[:9],
        up_grad,
        down_grad,
        hidden_grad,
        col_grads[9:],
        time_grad,
        map_grad,
        attn_grad,
        out_grad,
    )


def choose(latents, *rest):
    shape = {axis: lax.axis_size(axis) for axis in ("dp", "band")}
    fits = (
        shape["dp"] == 2 * PLANE
        and shape["band"] == LINE
        and latents.shape[0] == LINE
        and latents.shape[3] % (2 * PLANE * HEAD_DIM) == 0
    )
    return (paired_device if fits else per_device)(latents, *rest)


def solution(mesh):
    placed = (
        P("dp", "band", None, None),
        P("dp", None, None),
        P("dp", None),
        P("dp"),
        P(None, ("dp", "band")),
        P(("dp", "band"), None),
        P(("dp", "band"), None),
        P(None, ("dp", "band")),
        P(None, ("dp", "band")),
        P(None, ("dp", "band")),
        P(("dp", "band"), None),
        P(None, ("dp", "band"), None),
        P(("dp", "band"), None),
        P("dp", "band", None, None),
    )
    return jax.shard_map(
        choose,
        mesh=mesh,
        in_specs=placed,
        out_specs=(
            P("dp", "band", None, None),
            P("dp", "band", None, None),
            P("dp", None, "band"),
            P(None, ("dp", "band")),
            P(("dp", "band"), None),
            P(("dp", "band"), None),
            P(None, ("dp", "band")),
            P(None, ("dp", "band")),
            P(None, ("dp", "band")),
            P(("dp", "band"), None),
            P(None, ("dp", "band"), None),
            P(("dp", "band"), None),
        ),
        check_vma=False,
    )
```

```python
import functools

import jax
import jax.numpy as jnp
from jax import lax
from jax.experimental import pallas as pl
from jax.experimental.pallas import tpu as pltpu
from jax.sharding import PartitionSpec as P

HEAD_DIM = 64


def with_halo(array, sides, width):
    for axis, dim in sides:
        size, length = (lax.axis_size(axis), array.shape[dim])
        up = [(i, (i + 1) % size) for i in range(size - 1)]
        down = [(j, i) for i, j in up]
        last = lax.slice_in_dim(array, length - width, length, axis=dim)
        first = lax.slice_in_dim(array, 0, width, axis=dim)
        before = lax.ppermute(last, axis, up)
        after = lax.ppermute(first, axis, down)
        array = jnp.concatenate([before, array, after], axis=dim)
    return array


def product(left_op, right_op):
    return jnp.dot(left_op, right_op, preferred_element_type=jnp.float32)


def product_tn(left_op, right_op):
    return lax.dot_general(
        left_op, right_op, (((0,), (0,)), ((), ())), preferred_element_type=jnp.float32
    )


def product_nt(left_op, right_op):
    return lax.dot_general(
        left_op, right_op, (((1,), (1,)), ((), ())), preferred_element_type=jnp.float32
    )


def norm_parts(array_in):
    center = array_in - jnp.mean(array_in, axis=-1, keepdims=True)
    spread = jnp.mean(center * center, axis=-1, keepdims=True)
    inverse = lax.rsqrt(spread + 1e-06)
    return (center * inverse, inverse)


def norm_back(incoming, normed, inverse):
    return inverse * (
        incoming
        - jnp.mean(incoming, axis=-1, keepdims=True)
        - normed * jnp.mean(incoming * normed, axis=-1, keepdims=True)
    )


def column_sums(array_in):
    return jnp.sum(array_in.astype(jnp.float32), axis=0)


def gelu_exact(array_in):
    return jax.nn.gelu(array_in, approximate=False)


def masked_scores(query_one, key_one, valid_one):
    raw_scores = jnp.einsum(
        "qhd,khd->hqk", query_one, key_one, preferred_element_type=jnp.float32
    ) * HEAD_DIM ** (-0.5)
    return jnp.where(valid_one[None, None, :], raw_scores, -1000000000.0)


def attend_one(items):
    query_one, key_one, value_one, valid_one = items
    scores = masked_scores(query_one, key_one, valid_one)
    top_score = jnp.max(scores, axis=-1, keepdims=True)
    exponent = jnp.exp(scores - top_score)
    row_total = jnp.sum(exponent, axis=-1, keepdims=True)
    log_total = top_score + jnp.log(row_total)
    probs_low = (exponent / row_total).astype(jnp.bfloat16)
    mixed_one = jnp.einsum(
        "hqk,khd->qhd", probs_low, value_one, preferred_element_type=jnp.float32
    ).astype(jnp.bfloat16)
    return (mixed_one, log_total)


def attend_back(items):
    query_one, key_one, value_one, valid_one, log_one, gmix_one = items
    weights_again = jnp.exp(masked_scores(query_one, key_one, valid_one) - log_one)
    g_probs = jnp.einsum("qhd,khd->hqk", gmix_one, value_one, preferred_element_type=jnp.float32)
    inner_sum = jnp.sum(weights_again * g_probs, axis=-1, keepdims=True)
    g_score = (weights_again * (g_probs - inner_sum)).astype(jnp.bfloat16)
    probs_again = weights_again.astype(jnp.bfloat16)
    g_query = (
        jnp.einsum("hqk,khd->qhd", g_score, key_one, preferred_element_type=jnp.float32)
        * HEAD_DIM ** (-0.5)
    ).astype(jnp.bfloat16)
    g_key = jnp.einsum(
        "hqk,qhd->khd", g_score, query_one, preferred_element_type=jnp.float32
    ) * HEAD_DIM ** (-0.5)
    g_value = jnp.einsum("hqk,qhd->khd", probs_again, gmix_one, preferred_element_type=jnp.float32)
    return (g_query, g_key, g_value)


def per_device(
    latents,
    clip_text,
    embedding,
    lengths,
    conv_weight,
    up_weight,
    down_weight,
    hidden_vecs,
    vectors,
    time_weight,
    map_weight,
    attn_in,
    out_weight,
    grad_out,
):
    lat_count, band_rows, columns, channels = latents.shape
    tokens_lat = band_rows * columns
    tok_rows = lat_count * tokens_lat
    hidden_width = up_weight.shape[1]
    text_len = clip_text.shape[1]
    clip_width = clip_text.shape[2]
    band_size = lax.axis_size("band")
    band_index = lax.axis_index("band")
    pixel_count = tokens_lat * band_size
    head_count = channels // HEAD_DIM
    band_share = 1.0 / band_size
    res_shards = (conv_weight, up_weight, down_weight, hidden_vecs, vectors)
    attn_shards = (time_weight, map_weight, attn_in, out_weight)
    res_full = (
        lax.all_gather(res_shards[0], ("dp", "band"), axis=1, tiled=True),
        lax.all_gather(res_shards[1], ("dp", "band"), axis=0, tiled=True),
        lax.all_gather(res_shards[2], ("dp", "band"), axis=0, tiled=True),
        lax.all_gather(res_shards[3], ("dp", "band"), axis=1, tiled=True),
        lax.all_gather(res_shards[4], ("dp", "band"), axis=1, tiled=True),
    )
    attn_full = (
        lax.all_gather(attn_shards[0], ("dp", "band"), axis=1, tiled=True),
        lax.all_gather(attn_shards[1], ("dp", "band"), axis=0, tiled=True),
        lax.all_gather(attn_shards[2], ("dp", "band"), axis=1, tiled=True),
        lax.all_gather(attn_shards[3], ("dp", "band"), axis=0, tiled=True),
    )
    hidden_values = res_full[3].astype(jnp.float32)
    vec_values = res_full[4].astype(jnp.float32)
    framed = with_halo(latents, (("band", 1),), 1)
    framed = jnp.pad(framed, ((0, 0), (0, 0), (1, 1), (0, 0)))
    conv_taps = res_full[0].astype(jnp.float32)
    conv_out = jnp.broadcast_to(vec_values[0], latents.shape)
    for offset in range(9):
        row_shift = offset // 3
        col_shift = offset % 3
        conv_out = conv_out + conv_taps[offset] * framed[
            :, row_shift : row_shift + band_rows, col_shift : col_shift + columns
        ].astype(jnp.float32)
    first_norm, first_inv = norm_parts(conv_out.reshape(tok_rows, channels))
    first_in = first_norm.astype(jnp.bfloat16)
    up_out = product(first_in, res_full[1]) + hidden_values[0]
    active = gelu_exact(up_out)
    active_lat = active.reshape(lat_count, tokens_lat, hidden_width)
    square_sums = lax.psum(
        jnp.sum(active_lat * active_lat, axis=1).astype(jnp.bfloat16), "band"
    ).astype(jnp.float32)
    strength = jnp.sqrt(square_sums)
    grn_denom = jnp.mean(strength, axis=-1, keepdims=True) + 1e-06
    grn_ratio = strength / grn_denom
    gamma_vec = hidden_values[1]
    grn_out = (
        (gamma_vec * (active_lat * grn_ratio[:, None]) + hidden_values[2] + active_lat)
        .astype(jnp.bfloat16)
        .reshape(tok_rows, hidden_width)
    )
    first_sum = latents.reshape(tok_rows, channels).astype(jnp.float32) + (
        product(grn_out, res_full[2]) + vec_values[1]
    )
    modulation = product(embedding, attn_full[0])
    scale_vec = modulation[:, :channels] + vec_values[2]
    shift_vec = modulation[:, channels:] + vec_values[3]
    first_lat = first_sum.reshape(lat_count, tokens_lat, channels)
    second = first_lat * (1.0 + scale_vec[:, None]) + shift_vec[:, None]
    second_norm, second_inv = norm_parts(second)
    second_in = second_norm.astype(jnp.bfloat16).reshape(tok_rows, channels)
    clip_words = (
        jax.nn.silu(clip_text.astype(jnp.float32))
        .astype(jnp.bfloat16)
        .reshape(lat_count * text_len, clip_width)
    )
    mapped = (product(clip_words, attn_full[1]) + vec_values[4]).astype(jnp.bfloat16)
    projections = attn_full[2]
    query_rows = (product(second_in, projections[0]) + vec_values[5]).astype(jnp.bfloat16)
    pixel_key = (
        product(second_in, projections[1])
        .astype(jnp.bfloat16)
        .reshape(lat_count, tokens_lat, channels)
    )
    pixel_value = (
        (product(second_in, projections[2]) + vec_values[6])
        .astype(jnp.bfloat16)
        .reshape(lat_count, tokens_lat, channels)
    )
    all_key, all_value = (
        lax.all_gather(pixel_key, "band", axis=1, tiled=True),
        lax.all_gather(pixel_value, "band", axis=1, tiled=True),
    )
    text_key = (
        product(mapped, projections[1]).astype(jnp.bfloat16).reshape(lat_count, text_len, channels)
    )
    text_value = (
        (product(mapped, projections[2]) + vec_values[6])
        .astype(jnp.bfloat16)
        .reshape(lat_count, text_len, channels)
    )
    key_rows = jnp.concatenate([all_key, text_key], axis=1).reshape(
        lat_count, pixel_count + text_len, head_count, HEAD_DIM
    )
    value_rows = jnp.concatenate([all_value, text_value], axis=1).reshape(
        lat_count, pixel_count + text_len, head_count, HEAD_DIM
    )
    query_heads = query_rows.reshape(lat_count, tokens_lat, head_count, HEAD_DIM)
    key_places = jnp.arange(pixel_count + text_len, dtype=jnp.int32)
    valid_keys = key_places[None, :] < pixel_count + lengths[:, None]
    mixed_heads, log_totals = lax.map(attend_one, (query_heads, key_rows, value_rows, valid_keys))
    mixed_out = mixed_heads.reshape(tok_rows, channels)
    attended = product(mixed_out, attn_full[3]) + vec_values[7]
    layer_out = (
        (second.reshape(tok_rows, channels) + attended).astype(jnp.bfloat16).reshape(latents.shape)
    )
    res_back = (
        lax.all_gather(res_shards[0], ("dp", "band"), axis=1, tiled=True),
        lax.all_gather(res_shards[1], ("dp", "band"), axis=0, tiled=True),
        lax.all_gather(res_shards[2], ("dp", "band"), axis=0, tiled=True),
        lax.all_gather(res_shards[3], ("dp", "band"), axis=1, tiled=True),
        lax.all_gather(res_shards[4], ("dp", "band"), axis=1, tiled=True),
    )
    attn_back = (
        lax.all_gather(attn_shards[0], ("dp", "band"), axis=1, tiled=True),
        lax.all_gather(attn_shards[1], ("dp", "band"), axis=0, tiled=True),
        lax.all_gather(attn_shards[2], ("dp", "band"), axis=1, tiled=True),
        lax.all_gather(attn_shards[3], ("dp", "band"), axis=0, tiled=True),
    )
    proj_back = attn_back[2]
    grad_rows = grad_out.reshape(tok_rows, channels)
    grad_float = grad_rows.astype(jnp.float32)
    out_grad_w = product_tn(mixed_out, grad_rows)
    g_mixed = (
        product_nt(grad_rows, attn_back[3])
        .astype(jnp.bfloat16)
        .reshape(lat_count, tokens_lat, head_count, HEAD_DIM)
    )
    g_query_heads, g_key, g_value = lax.map(
        attend_back, (query_heads, key_rows, value_rows, valid_keys, log_totals, g_mixed)
    )
    g_query = g_query_heads.reshape(tok_rows, channels)
    g_key = g_key.reshape(lat_count, pixel_count + text_len, channels)
    g_value = g_value.reshape(lat_count, pixel_count + text_len, channels)
    pixel_gkey, pixel_gvalue = (
        lax.psum_scatter(
            g_key[:, :pixel_count].astype(jnp.bfloat16), "band", scatter_dimension=1, tiled=True
        ).astype(jnp.float32),
        lax.psum_scatter(
            g_value[:, :pixel_count].astype(jnp.bfloat16), "band", scatter_dimension=1, tiled=True
        ).astype(jnp.float32),
    )
    text_gkey, text_gvalue = (
        lax.psum(g_key[:, pixel_count:].astype(jnp.bfloat16), "band").astype(jnp.float32),
        lax.psum(g_value[:, pixel_count:].astype(jnp.bfloat16), "band").astype(jnp.float32),
    )
    pixel_kb = pixel_gkey.astype(jnp.bfloat16).reshape(tok_rows, channels)
    pixel_vb = pixel_gvalue.astype(jnp.bfloat16).reshape(tok_rows, channels)
    text_kb = text_gkey.astype(jnp.bfloat16).reshape(lat_count * text_len, channels)
    text_vb = text_gvalue.astype(jnp.bfloat16).reshape(lat_count * text_len, channels)
    g_second_in = (
        product_nt(g_query, proj_back[0])
        + product_nt(pixel_kb, proj_back[1])
        + product_nt(pixel_vb, proj_back[2])
    )
    grad_query_w = product_tn(second_in, g_query)
    grad_key_w = product_tn(second_in, pixel_kb) + band_share * product_tn(mapped, text_kb)
    grad_value_w = product_tn(second_in, pixel_vb) + band_share * product_tn(mapped, text_vb)
    g_mapped = (product_nt(text_kb, proj_back[1]) + product_nt(text_vb, proj_back[2])).astype(
        jnp.bfloat16
    )
    grad_map_w = band_share * product_tn(clip_words, g_mapped)
    clip_slice = clip_width // band_size
    map_rows = lax.dynamic_slice_in_dim(attn_back[1], band_index * clip_slice, clip_slice, 0)
    text_part = lax.dynamic_slice_in_dim(clip_text, band_index * clip_slice, clip_slice, 2).astype(
        jnp.float32
    )
    sigmoid_text = jax.nn.sigmoid(text_part)
    g_words = product_nt(g_mapped, map_rows).reshape(lat_count, text_len, clip_slice)
    text_grad = (g_words * (sigmoid_text * (1.0 + text_part * (1.0 - sigmoid_text)))).astype(
        jnp.bfloat16
    )
    g_second = grad_float.reshape(lat_count, tokens_lat, channels) + norm_back(
        g_second_in.reshape(lat_count, tokens_lat, channels), second_norm, second_inv
    )
    g_scale = jnp.sum(g_second * first_lat, axis=1)
    g_shift = jnp.sum(g_second, axis=1)
    grad_time_w = lax.dot_general(
        embedding.astype(jnp.float32),
        jnp.concatenate([g_scale, g_shift], axis=1),
        (((0,), (0,)), ((), ())),
        precision=lax.Precision.HIGHEST,
        preferred_element_type=jnp.float32,
    )
    attn_grads = (
        lax.psum_scatter(grad_time_w, ("dp", "band"), scatter_dimension=1, tiled=True),
        lax.psum_scatter(grad_map_w, ("dp", "band"), scatter_dimension=0, tiled=True),
        lax.psum_scatter(
            jnp.stack([grad_query_w, grad_key_w, grad_value_w]),
            ("dp", "band"),
            scatter_dimension=1,
            tiled=True,
        ),
        lax.psum_scatter(out_grad_w, ("dp", "band"), scatter_dimension=0, tiled=True),
    )
    g_first = g_second * (1.0 + scale_vec[:, None])
    g_down = g_first.astype(jnp.bfloat16).reshape(tok_rows, channels)
    grad_down_w = product_tn(grn_out, g_down)
    g_grn = product_nt(g_down, res_back[2]).reshape(lat_count, tokens_lat, hidden_width)
    grad_gamma = jnp.sum(g_grn * active_lat * grn_ratio[:, None], axis=(0, 1))
    grad_beta = jnp.sum(g_grn, axis=(0, 1))
    g_ratio = lax.psum(
        jnp.sum(g_grn * gamma_vec * active_lat, axis=1).astype(jnp.bfloat16), "band"
    ).astype(jnp.float32)
    g_strength = g_ratio / grn_denom - jnp.sum(g_ratio * strength, axis=-1, keepdims=True) / (
        hidden_width * grn_denom * grn_denom
    )
    g_active = (
        g_grn * (1.0 + gamma_vec * grn_ratio[:, None])
        + active_lat * (g_strength / strength)[:, None]
    )
    gelu_value, gelu_pull = jax.vjp(gelu_exact, up_out)
    g_up = gelu_pull(g_active.reshape(tok_rows, hidden_width))[0].astype(jnp.bfloat16)
    grad_up_w = product_tn(first_in, g_up)
    g_conv = (
        norm_back(product_nt(g_up, res_back[1]), first_norm, first_inv)
        .astype(jnp.bfloat16)
        .reshape(latents.shape)
    )
    g_framed = with_halo(g_conv, (("band", 1),), 1)
    g_framed = jnp.pad(g_framed, ((0, 0), (0, 0), (1, 1), (0, 0)))
    conv_back = res_back[0].astype(jnp.float32)
    g_conv_f = g_conv.astype(jnp.float32)
    back_sum = g_first.reshape(latents.shape)
    tap_grads = []
    for offset in range(9):
        row_shift = offset // 3
        col_shift = offset % 3
        window = framed[
            :, row_shift : row_shift + band_rows, col_shift : col_shift + columns
        ].astype(jnp.float32)
        tap_grads.append(jnp.sum(g_conv_f * window, axis=(0, 1, 2)))
        back_sum = back_sum + conv_back[offset] * g_framed[
            :, 2 - row_shift : 2 - row_shift + band_rows, 2 - col_shift : 2 - col_shift + columns
        ].astype(jnp.float32)
    latent_grad = back_sum.astype(jnp.bfloat16)
    grad_vectors = jnp.stack(
        [
            jnp.sum(g_conv_f, axis=(0, 1, 2)),
            column_sums(g_down),
            jnp.sum(g_scale, axis=0),
            jnp.sum(g_shift, axis=0),
            band_share * column_sums(g_mapped),
            column_sums(g_query),
            column_sums(pixel_vb) + band_share * column_sums(text_vb),
            jnp.sum(grad_float, axis=0),
        ]
    )
    grad_hidden = jnp.stack([column_sums(g_up), grad_gamma, grad_beta])
    grad_conv_w = jnp.stack(tap_grads)
    res_grads = (
        lax.psum_scatter(grad_conv_w, ("dp", "band"), scatter_dimension=1, tiled=True),
        lax.psum_scatter(grad_up_w, ("dp", "band"), scatter_dimension=0, tiled=True),
        lax.psum_scatter(grad_down_w, ("dp", "band"), scatter_dimension=0, tiled=True),
        lax.psum_scatter(grad_hidden, ("dp", "band"), scatter_dimension=1, tiled=True),
        lax.psum_scatter(grad_vectors, ("dp", "band"), scatter_dimension=1, tiled=True),
    )
    return (
        layer_out,
        latent_grad,
        text_grad,
        res_grads[0],
        res_grads[1],
        res_grads[2],
        res_grads[3],
        res_grads[4],
        attn_grads[0],
        attn_grads[1],
        attn_grads[2],
        attn_grads[3],
    )


PLANE = 4
LINE = 4
PAIR = 2 * HEAD_DIM


def key_bias(length, keys, pixels):
    rows = lax.broadcasted_iota(jnp.int32, (keys, 1), 0)
    return jnp.where(rows < pixels + length, 0.0, -1000000000.0)


def one_head(value, head):
    lanes = lax.broadcasted_iota(jnp.int32, value.shape, 1)
    return jnp.where((lanes // HEAD_DIM) == head, value, jnp.zeros_like(value))


def attend_kernel(pixels, length_ref, rows_ref, mixed_ref, log_ref):
    keys = rows_ref.shape[1]
    bias = key_bias(length_ref[pl.program_id(0)], keys, pixels)
    query = rows_ref[0, :pixels, :PAIR] * HEAD_DIM ** (-0.5)
    key = rows_ref[0, :, PAIR : 2 * PAIR]
    value = rows_ref[0, :, 2 * PAIR :]
    total = jnp.zeros((pixels, PAIR), jnp.float32)
    for head in range(PAIR // HEAD_DIM):
        scores = product_nt(key, one_head(query, head)) + bias
        top = jnp.max(scores, axis=0, keepdims=True)
        exponent = jnp.exp(scores - top)
        row_total = jnp.sum(exponent, axis=0, keepdims=True)
        probs = (exponent * (1.0 / row_total)).astype(jnp.bfloat16)
        total = total + product_tn(probs, one_head(value, head))
        log_ref[0, 0, head : head + 1, :] = top + jnp.log(row_total)
    mixed_ref[0] = total.astype(jnp.bfloat16)


def attend_back_kernel(pixels, length_ref, rows_ref, gmix_ref, log_ref, grad_ref):
    keys = rows_ref.shape[1]
    bias = key_bias(length_ref[pl.program_id(0)], keys, pixels)
    query = rows_ref[0, :pixels, :PAIR] * HEAD_DIM ** (-0.5)
    key = rows_ref[0, :, PAIR : 2 * PAIR]
    value = rows_ref[0, :, 2 * PAIR :]
    g_query = jnp.zeros((pixels, PAIR), jnp.float32)
    g_key = jnp.zeros((keys, PAIR), jnp.float32)
    g_value = jnp.zeros((keys, PAIR), jnp.float32)
    for head in range(PAIR // HEAD_DIM):
        query_one = one_head(query, head)
        gmix_one = one_head(gmix_ref[0], head)
        scores = product_nt(key, query_one) + bias
        weights = jnp.exp(scores - log_ref[0, 0, head : head + 1, :])
        g_probs = product_nt(value, gmix_one)
        inner = jnp.sum(weights * g_probs, axis=0, keepdims=True)
        g_score = (weights * (g_probs - inner)).astype(jnp.bfloat16)
        g_key = g_key + product(g_score, query_one)
        g_value = g_value + product(weights.astype(jnp.bfloat16), gmix_one)
        g_query = g_query + product_tn(g_score, one_head(key, head))
    g_query = (g_query * HEAD_DIM ** (-0.5)).astype(jnp.bfloat16)
    grad_ref[0, :pixels, :PAIR] = g_query
    grad_ref[0, pixels:, :PAIR] = jnp.zeros((keys - pixels, PAIR), jnp.bfloat16)
    grad_ref[0, :, PAIR : 2 * PAIR] = g_key.astype(jnp.bfloat16)
    grad_ref[0, :, 2 * PAIR :] = g_value.astype(jnp.bfloat16)


def attend_specs(keys, pixels):
    rows = pl.BlockSpec((1, keys, 3 * PAIR), lambda i, j, n: (i, 0, j))
    narrow = pl.BlockSpec((1, pixels, PAIR), lambda i, j, n: (i, 0, j))
    logs = pl.BlockSpec((1, 1, PAIR // HEAD_DIM, pixels), lambda i, j, n: (i, j, 0, 0))
    return (rows, narrow, logs)


def attend(rows, lengths, pixels):
    count, keys, width = rows.shape
    groups = width // (3 * PAIR)
    rows_spec, narrow, logs = attend_specs(keys, pixels)
    return pl.pallas_call(
        functools.partial(attend_kernel, pixels),
        out_shape=(
            jax.ShapeDtypeStruct((count, pixels, groups * PAIR), jnp.bfloat16),
            jax.ShapeDtypeStruct((count, groups, PAIR // HEAD_DIM, pixels), jnp.float32),
        ),
        grid_spec=pltpu.PrefetchScalarGridSpec(
            num_scalar_prefetch=1,
            grid=(count, groups),
            in_specs=[rows_spec],
            out_specs=[narrow, logs],
        ),
        compiler_params=pltpu.CompilerParams(vmem_limit_bytes=40 << 20),
        cost_estimate=pl.CostEstimate(
            flops=count * groups * 8 * pixels * keys * PAIR,
            bytes_accessed=rows.size * 3,
            transcendentals=2 * count * groups * pixels * keys,
        ),
        name="attend",
    )(lengths, rows)


def attend_back_pairs(rows, g_mixed, logs_in, lengths, pixels):
    count, keys, width = rows.shape
    groups = width // (3 * PAIR)
    rows_spec, narrow, logs = attend_specs(keys, pixels)
    return pl.pallas_call(
        functools.partial(attend_back_kernel, pixels),
        out_shape=jax.ShapeDtypeStruct(rows.shape, jnp.bfloat16),
        grid_spec=pltpu.PrefetchScalarGridSpec(
            num_scalar_prefetch=1,
            grid=(count, groups),
            in_specs=[rows_spec, narrow, logs],
            out_specs=rows_spec,
        ),
        compiler_params=pltpu.CompilerParams(vmem_limit_bytes=40 << 20),
        cost_estimate=pl.CostEstimate(
            flops=count * groups * 20 * pixels * keys * PAIR,
            bytes_accessed=rows.size * 5,
            transcendentals=2 * count * groups * pixels * keys,
        ),
        name="attend_back",
    )(lengths, rows, g_mixed, logs_in)


def swap(value, bit):
    return lax.ppermute(value, "dp", [(i, i ^ bit) for i in range(2 * PLANE)])


def rotate(value, step):
    return lax.ppermute(value, "band", [(i, (i + step) % LINE) for i in range(LINE)])


def pick(value, index, axis=0):
    return lax.dynamic_index_in_dim(value, index, axis, keepdims=False)


def put(buffer, value, index, axis=0):
    return lax.dynamic_update_index_in_dim(buffer, value, index, axis)


def spread_line(blocks, place):
    result = jnp.zeros(blocks.shape, blocks.dtype)
    result = put(result, pick(blocks, place), place)
    for step in range(1, LINE):
        moved = rotate(pick(blocks, (place + step) % LINE), step)
        result = put(result, moved, (place - step) % LINE)
    return result


def gather_line(shard, place):
    parts, rows, cols = shard.shape
    result = jnp.zeros((parts, LINE, rows, cols), shard.dtype)
    result = put(result, shard, place, 1)
    for step in range(1, LINE):
        result = put(result, rotate(shard, step), (place - step) % LINE, 1)
    return result


def gather_plane(block, plane):
    rows, cols = block.shape
    half = rows // 2
    by_x, by_y = (swap(block, 2), swap(block, 4))
    upper = swap(by_y[:half], 2)
    lower = swap(by_x[half:], 4)
    result = jnp.zeros((PLANE, rows, cols), block.dtype)
    result = put(result, block, plane)
    result = put(result, by_x, plane ^ 1)
    result = put(result, by_y, plane ^ 2)
    zero = jnp.int32(0)
    result = lax.dynamic_update_slice(result, upper[None], (plane ^ 3, zero, zero))
    result = lax.dynamic_update_slice(result, lower[None], (plane ^ 3, zero + half, zero))
    return (result, (by_x, by_y))


def held(*values):
    return lax.optimization_barrier(values)


def flat_line(shard, place):
    parts, rows, cols = shard.shape
    return gather_line(shard, place).reshape(parts * LINE * rows, cols)


def flat_plane(line, plane):
    full, _ = gather_plane(line, plane)
    return full.reshape(-1, line.shape[1])


def reduce_owner(pieces, parts, plane, place):
    low = jnp.bfloat16
    first, second, last = pieces
    far = [first(plane ^ 3, half).astype(low) for half in range(2)]
    via_x, via_y = (swap(far[0], 2), swap(far[1], 4))
    out_x = [second(plane ^ 1, 0).astype(low), None]
    out_y = [None, second(plane ^ 2, 1).astype(low)]
    got_x, got_y = ([swap(out_x[0], 2), None], [None, swap(out_y[1], 4)])
    out_x[1] = (second(plane ^ 1, 1) + via_y.astype(jnp.float32)).astype(low)
    out_y[0] = (second(plane ^ 2, 0) + via_x.astype(jnp.float32)).astype(low)
    got_x[1], got_y[0] = (swap(out_x[1], 2), swap(out_y[0], 4))
    results = []
    for half in range(2):
        total = (
            last(plane, half)
            + got_x[half].astype(jnp.float32)
            + got_y[half].astype(jnp.float32)
        )
        rows, cols = total.shape
        total = total.reshape(parts, LINE, rows // (parts * LINE), cols)
        summed = pick(total, place, 1)
        for step in range(1, LINE):
            sent = pick(total, (place + step) % LINE, 1).astype(low)
            summed = summed + rotate(sent, step).astype(jnp.float32)
        results.append(summed)
    return jnp.concatenate(results, axis=-1)


def gather_small(value, plane, core, place):
    cores = jnp.zeros((2,) + value.shape, value.dtype)
    cores = put(put(cores, value, core), swap(value, 1), 1 - core)
    full = gather_small_plane(cores, plane)
    line = jnp.zeros((LINE,) + full.shape, value.dtype)
    line = put(line, full, place)
    for step in range(1, LINE):
        line = put(line, rotate(full, step), (place - step) % LINE)
    return line


def gather_small_plane(line, plane):
    by_x = swap(line, 2)
    both = jnp.stack([line, by_x])
    by_y = swap(both, 4)
    full = jnp.zeros((PLANE,) + line.shape, line.dtype)
    full = put(put(full, line, plane), by_x, plane ^ 1)
    return put(put(full, by_y[0], plane ^ 2), by_y[1], plane ^ 3)


def reduce_small(value, plane, place):
    both = jnp.stack([pick(value, plane ^ 1), pick(value, plane ^ 3)])
    by_x = swap(both, 2)
    mine = pick(value, plane) + by_x[0]
    other = pick(value, plane ^ 2) + by_x[1]
    mine = mine + swap(other, 4)
    summed = pick(mine, place)
    for step in range(1, LINE):
        summed = summed + rotate(pick(mine, (place + step) % LINE), step)
    return summed


def pair(value):
    return jnp.stack([value, swap(value, 1)])


def pair_sum(value):
    return value + swap(value, 1)[::-1]


def own_sum(own, partner):
    return own + swap(partner.astype(jnp.bfloat16), 1).astype(jnp.float32)


def core_half(value, axis, core, chips=PLANE):
    shape = value.shape
    split = shape[:axis] + (chips, 2, shape[axis] // (2 * chips)) + shape[axis + 1 :]
    half = pick(value.reshape(split), core, axis + 1)
    return half.reshape(shape[:axis] + (shape[axis] // 2,) + shape[axis + 1 :])


def core_merge(own, other, axis, core):
    shape = own.shape
    split = shape[:axis] + (PLANE, 1, shape[axis] // PLANE) + shape[axis + 1 :]
    own, other = (own.reshape(split), other.reshape(split))
    first = jnp.where(core == 0, own, other)
    second = jnp.where(core == 0, other, own)
    merged = jnp.concatenate([first, second], axis=axis + 1)
    return merged.reshape(shape[:axis] + (2 * shape[axis],) + shape[axis + 1 :])


def paired_device(
    latents,
    clip_text,
    embedding,
    lengths,
    conv_weight,
    up_weight,
    down_weight,
    hidden_vecs,
    vectors,
    time_weight,
    map_weight,
    attn_in,
    out_weight,
    grad_out,
):
    lat_count, band_rows, columns, channels = latents.shape
    height = band_rows * LINE
    pixels = height * columns
    text_len, clip_width = clip_text.shape[1:]
    hidden_width = up_weight.shape[1]
    time_rank = time_weight.shape[0]
    half_channels, half_hidden = (channels // 2, hidden_width // 2)
    dp_index = lax.axis_index("dp")
    place = lax.axis_index("band")
    plane, core = (dp_index // 2, dp_index % 2)
    f32, low = (jnp.float32, jnp.bfloat16)

    small = jnp.concatenate(
        [
            conv_weight.reshape(-1),
            vectors.reshape(-1),
            hidden_vecs.reshape(-1),
            time_weight.reshape(-1),
        ]
    )
    col_rows, col_width = (9 + vectors.shape[0], conv_weight.shape[1])
    def with_partner(value, axis):
        kept = core_half(value, axis, core)
        got = swap(core_half(value, axis, 1 - core), 1)
        both = jnp.zeros((2,) + kept.shape, kept.dtype)
        return put(put(both, kept, core), got, 1 - core)

    def attn_order(value):
        groups = jnp.moveaxis(value.reshape(value.shape[:-1] + (-1, PAIR)), 0, -2)
        return groups.reshape(groups.shape[:-3] + (-1,))

    def attn_back_order(value):
        groups = jnp.moveaxis(value.reshape(value.shape[:-1] + (-1, 3, PAIR)), -2, 0)
        return groups.reshape(groups.shape[:-2] + (-1,))

    up_shard = with_partner(up_weight, 1)
    up_shard, small, latents_held = held(up_shard, small, latents)
    latent = spread_line(latents_held, place).reshape(height, columns, channels)
    up_line = flat_line(up_shard, place)
    small_all = gather_small(small, plane, core, place)
    up_line, latent, small_all, clip_text, attn_in, embedding = held(
        up_line, latent, small_all, clip_text, attn_in, embedding
    )
    up_full = flat_plane(up_line, plane)
    small_all, time_low = (small_all.astype(f32), small_all)
    col_all = small_all[..., : col_rows * col_width]
    col_all = col_all.reshape(LINE, PLANE, 2, col_rows, col_width).transpose(3, 1, 2, 0, 4)
    col_all = col_all.reshape(col_rows, channels)
    taps, vecs = (col_all[:9], col_all[9:])
    time_at = col_rows * col_width + hidden_vecs.size
    hidden_all = pick(small_all[..., col_rows * col_width : time_at], core, 2)
    hidden_all = hidden_all.reshape(LINE, PLANE, 3, -1).transpose(2, 1, 0, 3)
    hidden_all = hidden_all.reshape(3, half_hidden)

    time_all = time_low[..., time_at:].reshape(LINE, PLANE, 2, time_rank, -1)
    time_all = time_all.transpose(3, 1, 2, 0, 4).reshape(time_rank, 2 * channels)

    framed = jnp.pad(latent, ((1, 1), (1, 1), (0, 0)))
    conv_out = jnp.broadcast_to(vecs[0], latent.shape)
    for offset in range(9):
        row_shift, col_shift = (offset // 3, offset % 3)
        conv_out = conv_out + taps[offset] * framed[
            row_shift : row_shift + height, col_shift : col_shift + columns
        ].astype(f32)
    first_norm, first_inv = norm_parts(conv_out.reshape(pixels, channels))
    first_in = pair(first_norm.astype(low)).reshape(2 * pixels, channels)
    first_in, down_shard, mixed_shard = held(
        first_in, down_weight[None], jnp.concatenate([map_weight, out_weight])[None]
    )
    down_line = flat_line(down_shard, place)
    mixed_line = flat_line(mixed_shard, place)
    up_full, down_line, mixed_line, first_in, attn_in, clip_text = held(
        up_full, down_line, mixed_line, first_in, attn_in, clip_text
    )
    down_full = flat_plane(down_line, plane)
    up_out = product(first_in, up_full) + hidden_all[0]
    below = 0.5 + 0.5 * lax.erf(up_out * 0.5**0.5)
    slope = below + up_out * ((0.5 / jnp.pi) ** 0.5 * jnp.exp(-0.5 * up_out * up_out))
    active, slope = held((up_out * below).astype(low), slope.astype(low))
    active_lat = active.reshape(2, pixels, half_hidden).astype(f32)
    strength = jnp.sqrt(jnp.sum(active_lat * active_lat, axis=1))
    strength_sum = pair_sum(jnp.sum(strength, axis=-1, keepdims=True))
    grn_denom = strength_sum / hidden_width + 1e-06
    grn_ratio = strength / grn_denom
    gamma_vec = hidden_all[1]
    grn_out = (
        gamma_vec * (active_lat * grn_ratio[:, None]) + hidden_all[2] + active_lat
    ).astype(low)
    grn_out, attn_in = held(grn_out, attn_in)
    attn_shard = attn_order(jnp.moveaxis(with_partner(attn_in, 2), 1, 0))
    attn_line = flat_line(attn_shard, place)
    grn_out, down_full, attn_line, mixed_line, clip_text = held(
        grn_out, down_full, attn_line, mixed_line, clip_text
    )
    mixed_full = flat_plane(mixed_line, plane).reshape(PLANE * LINE, -1, channels)
    map_rows = map_weight.shape[0]
    map_full = mixed_full[:, :map_rows].reshape(-1, channels)
    out_full = mixed_full[:, map_rows:].reshape(-1, channels)
    attn_full = flat_plane(attn_line, plane)
    lowered = own_sum(product(grn_out[0], down_full), product(grn_out[1], down_full))
    first_sum = latent.reshape(pixels, channels).astype(f32) + (lowered + vecs[1])
    embed_own = pick(embedding, place)
    modulation = product(embed_own[None], time_all)[0]
    scale_vec = modulation[:channels] + vecs[2]
    shift_vec = modulation[channels:] + vecs[3]
    second = first_sum * (1.0 + scale_vec) + shift_vec
    second_norm, second_inv = norm_parts(second)
    clip_own = pick(clip_text, place).astype(f32)
    words_own = jax.nn.silu(clip_own).astype(low)
    text_pad = -(-text_len // 16) * 16
    words_own = jnp.pad(words_own, ((0, text_pad - text_len), (0, 0)))
    words = pair(words_own).reshape(2 * text_pad, clip_width)
    words_half = core_half(words, 1, core)
    lengths_two = pair(pick(lengths, place))
    mapped = pair_sum(product(words_half, map_full).reshape(2, text_pad, channels))
    mapped = (mapped + vecs[4]).astype(low)
    sources = jnp.concatenate([pair(second_norm.astype(low)), mapped], axis=1)
    keys = pixels + text_pad
    sources, attn_full, out_full, grad_shard = held(sources, attn_full, out_full, grad_out)
    sources = sources.reshape(2 * keys, channels)
    grad_own = spread_line(grad_shard, place).reshape(pixels, channels)
    bias = jnp.stack([vecs[5], jnp.zeros((channels,), f32), vecs[6]])
    bias = attn_order(core_half(bias, 1, core))
    rows_qkv = (product(sources, attn_full) + bias).astype(low)
    rows_qkv = rows_qkv.reshape(2, keys, 3 * half_channels)
    mixed, log_totals = attend(rows_qkv, lengths_two, pixels)
    attended = own_sum(product(mixed[0], out_full), product(mixed[1], out_full))
    layer_own = (second + (attended + vecs[7])).astype(low)
    grad_two = pair(grad_own)
    g_mixed = product_nt(grad_two.reshape(2 * pixels, channels), out_full).astype(low)
    g_mixed = g_mixed.reshape(2, pixels, half_channels)

    def owner_sums(left, right, parts, *gates):
        block = left.shape[1] // PLANE
        half = right.shape[1] // 2

        def pieces_of(left_op, right_op):
            def piece(chip, which):
                taken = lax.dynamic_slice_in_dim(left_op, chip * block, block, 1)
                return product_tn(taken, right_op[:, which * half : (which + 1) * half])

            return piece

        pieces = [pieces_of(left, right)]
        for gate in gates:
            left, right, _ = held(left, right, gate)
            pieces.append(pieces_of(left, right))
        pieces += [pieces[-1]] * (3 - len(pieces))
        return reduce_owner(pieces, parts, plane, place)

    g_rows = attend_back_pairs(rows_qkv, g_mixed, log_totals, lengths_two, pixels)
    g_second_in = own_sum(
        product_nt(g_rows[0, :pixels], attn_full), product_nt(g_rows[1, :pixels], attn_full)
    )
    out_grad = owner_sums(
        mixed.reshape(2 * pixels, half_channels),
        grad_two.reshape(2 * pixels, channels),
        1,
        g_rows,
        g_second_in,
    )[0]
    g_second_in, g_rows = held(g_second_in, g_rows)
    g_flat = g_rows.reshape(2 * keys, 3 * half_channels)
    grad_float = grad_own.astype(f32)
    g_second = grad_float + norm_back(g_second_in, second_norm, second_inv)
    g_scale = jnp.sum(g_second * first_sum, axis=0)
    g_shift = jnp.sum(g_second, axis=0)
    g_modulation = jnp.concatenate([g_scale, g_shift])
    time_part = embed_own.astype(f32)[:, None] * g_modulation[None]
    g_first = g_second * (1.0 + scale_vec)
    g_down_own = g_first.astype(low)
    g_down = pair(g_down_own).reshape(2 * pixels, channels)
    g_grn = product_nt(g_down, down_full).reshape(2, pixels, half_hidden)
    g_grn_active = jnp.sum(g_grn * active_lat, axis=1)
    g_grn_sum = jnp.sum(g_grn, axis=(0, 1))
    g_grn, g_grn_active, grad_beta = held(g_grn.astype(low), g_grn_active, g_grn_sum)
    g_grn_low = g_grn
    g_grn = g_grn.astype(f32)
    grad_gamma = jnp.sum(g_grn_active * grn_ratio, axis=0)
    g_ratio = g_grn_active * gamma_vec
    ratio_sum = pair_sum(jnp.sum(g_ratio * strength, axis=-1, keepdims=True))
    g_strength = g_ratio / grn_denom - ratio_sum / (hidden_width * grn_denom * grn_denom)
    g_active = (
        g_grn * (1.0 + gamma_vec * grn_ratio[:, None])
        + active_lat * (g_strength / strength)[:, None]
    )
    g_up = (g_active.reshape(2 * pixels, half_hidden) * slope.astype(f32)).astype(low)
    attn_grad = owner_sums(sources, g_flat, 2, g_down, g_grn_low)
    down_grad = owner_sums(
        grn_out.reshape(2 * pixels, half_hidden), g_down, 1, g_grn_low, g_up
    )[0]
    layer_own, g_text, _ = held(layer_own, g_rows[:, pixels:], g_down)
    layer_out = spread_line(layer_own.reshape(latents.shape), place)
    g_text = g_text.reshape(2 * text_pad, 3 * half_channels)
    g_mapped = pair_sum(product_nt(g_text, attn_full).reshape(2, text_pad, channels))
    g_mapped = g_mapped.astype(low).reshape(2 * text_pad, channels)
    map_grad = owner_sums(words_half, g_mapped, 1, g_grn_low, g_up)[0]
    g_words = product_nt(g_mapped, map_full).reshape(2, text_pad, -1)[:, :text_len]
    g_words = core_merge(g_words[0], swap(g_words[1], 1), 1, core)
    sigmoid_text = jax.nn.sigmoid(clip_own)
    text_own = (g_words * (sigmoid_text * (1.0 + clip_own * (1.0 - sigmoid_text)))).astype(low)
    text_own = text_own.reshape(text_len, LINE, clip_width // LINE).transpose(1, 0, 2)
    text_grad = spread_line(text_own, place)
    g_first_in = own_sum(
        product_nt(g_up[:pixels], up_full), product_nt(g_up[pixels:], up_full)
    )
    g_conv = norm_back(g_first_in, first_norm, first_inv).astype(low).reshape(latent.shape)
    up_grad = owner_sums(first_in, g_up, 2, g_conv)
    g_framed = jnp.pad(g_conv, ((1, 1), (1, 1), (0, 0)))
    g_conv_f = g_conv.astype(f32)
    back_sum = g_first.reshape(latent.shape)
    tap_grads = []
    for offset in range(9):
        row_shift, col_shift = (offset // 3, offset % 3)
        window = framed[
            row_shift : row_shift + height, col_shift : col_shift + columns
        ].astype(f32)
        tap_grads.append(jnp.sum(g_conv_f * window, axis=(0, 1)))
        back_sum = back_sum + taps[offset] * g_framed[
            2 - row_shift : 2 - row_shift + height, 2 - col_shift : 2 - col_shift + columns
        ].astype(f32)
    latent_grad = spread_line(back_sum.astype(low).reshape(latents.shape), place)

    up_grad = core_merge(
        pick(up_grad, core), swap(pick(up_grad, 1 - core), 1), 1, core
    )
    attn_grad = core_merge(
        attn_back_order(pick(attn_grad, core)),
        attn_back_order(swap(pick(attn_grad, 1 - core), 1)),
        2,
        core,
    )
    column_grads = attn_back_order(column_sums(g_flat))
    own_zero = jnp.zeros((half_channels,), f32)
    vec_parts = jnp.stack(
        [
            jnp.sum(g_conv_f, axis=(0, 1)),
            column_sums(g_down_own),
            g_scale,
            g_shift,
            column_sums(g_mapped[:text_pad]),
            core_merge(column_grads[0], own_zero, 0, core),
            core_merge(column_grads[2], own_zero, 0, core),
            jnp.sum(grad_float, axis=0),
        ]
    )
    col_parts = jnp.concatenate([jnp.stack(tap_grads), vec_parts])
    col_parts = col_parts.reshape(col_parts.shape[0], PLANE, 2, LINE, -1).transpose(1, 2, 3, 0, 4)
    col_parts = col_parts.reshape(PLANE, 2, LINE, -1)
    time_part = time_part.reshape(time_rank, PLANE, 2, LINE, -1).transpose(1, 2, 3, 0, 4)
    time_part = time_part.reshape(PLANE, 2, LINE, -1)
    core_parts = jnp.concatenate([col_parts, time_part], axis=-1)
    core_sum = pick(core_parts, core, 1) + swap(pick(core_parts, 1 - core, 1), 1)
    hidden_parts = jnp.stack([column_sums(g_up), grad_gamma, grad_beta])
    hidden_parts = hidden_parts.reshape(3, PLANE, LINE, -1).transpose(1, 2, 0, 3)
    hidden_parts = hidden_parts.reshape(PLANE, LINE, -1)
    small_sum = reduce_small(
        jnp.concatenate([core_sum, hidden_parts], axis=-1), plane, place
    )
    col_size, time_size = (17 * (channels // 32), time_rank * (channels // 16))
    col_grads = small_sum[:col_size].reshape(17, -1)
    time_grad = small_sum[col_size : col_size + time_size].reshape(time_rank, -1)
    hidden_grad = small_sum[col_size + time_size :].reshape(3, -1)
    return (
        layer_out,
        latent_grad,
        text_grad,
        col_grads[:9],
        up_grad,
        down_grad,
        hidden_grad,
        col_grads[9:],
        time_grad,
        map_grad,
        attn_grad,
        out_grad,
    )


def choose(latents, *rest):
    shape = {axis: lax.axis_size(axis) for axis in ("dp", "band")}
    fits = (
        shape["dp"] == 2 * PLANE
        and shape["band"] == LINE
        and latents.shape[0] == LINE
        and latents.shape[3] % (2 * PLANE * HEAD_DIM) == 0
    )
    return (paired_device if fits else per_device)(latents, *rest)


def solution(mesh):
    placed = (
        P("dp", "band", None, None),
        P("dp", None, None),
        P("dp", None),
        P("dp"),
        P(None, ("dp", "band")),
        P(("dp", "band"), None),
        P(("dp", "band"), None),
        P(None, ("dp", "band")),
        P(None, ("dp", "band")),
        P(None, ("dp", "band")),
        P(("dp", "band"), None),
        P(None, ("dp", "band"), None),
        P(("dp", "band"), None),
        P("dp", "band", None, None),
    )
    return jax.shard_map(
        choose,
        mesh=mesh,
        in_specs=placed,
        out_specs=(
            P("dp", "band", None, None),
            P("dp", "band", None, None),
            P("dp", None, "band"),
            P(None, ("dp", "band")),
            P(("dp", "band"), None),
            P(("dp", "band"), None),
            P(None, ("dp", "band")),
            P(None, ("dp", "band")),
            P(None, ("dp", "band")),
            P(("dp", "band"), None),
            P(None, ("dp", "band"), None),
            P(("dp", "band"), None),
        ),
        check_vma=False,
    )
```

```python
import functools

import jax
import jax.numpy as jnp
from jax import lax
from jax.experimental import pallas as pl
from jax.experimental.pallas import tpu as pltpu
from jax.sharding import PartitionSpec as P

HEAD_DIM = 64


def with_halo(array, sides, width):
    for axis, dim in sides:
        size, length = (lax.axis_size(axis), array.shape[dim])
        up = [(i, (i + 1) % size) for i in range(size - 1)]
        down = [(j, i) for i, j in up]
        last = lax.slice_in_dim(array, length - width, length, axis=dim)
        first = lax.slice_in_dim(array, 0, width, axis=dim)
        before = lax.ppermute(last, axis, up)
        after = lax.ppermute(first, axis, down)
        array = jnp.concatenate([before, array, after], axis=dim)
    return array


def product(left_op, right_op):
    return jnp.dot(left_op, right_op, preferred_element_type=jnp.float32)


def product_tn(left_op, right_op):
    return lax.dot_general(
        left_op, right_op, (((0,), (0,)), ((), ())), preferred_element_type=jnp.float32
    )


def product_nt(left_op, right_op):
    return lax.dot_general(
        left_op, right_op, (((1,), (1,)), ((), ())), preferred_element_type=jnp.float32
    )


def norm_parts(array_in):
    center = array_in - jnp.mean(array_in, axis=-1, keepdims=True)
    spread = jnp.mean(center * center, axis=-1, keepdims=True)
    inverse = lax.rsqrt(spread + 1e-06)
    return (center * inverse, inverse)


def norm_back(incoming, normed, inverse):
    return inverse * (
        incoming
        - jnp.mean(incoming, axis=-1, keepdims=True)
        - normed * jnp.mean(incoming * normed, axis=-1, keepdims=True)
    )


def column_sums(array_in):
    return jnp.sum(array_in.astype(jnp.float32), axis=0)


def gelu_exact(array_in):
    return jax.nn.gelu(array_in, approximate=False)


def masked_scores(query_one, key_one, valid_one):
    raw_scores = jnp.einsum(
        "qhd,khd->hqk", query_one, key_one, preferred_element_type=jnp.float32
    ) * HEAD_DIM ** (-0.5)
    return jnp.where(valid_one[None, None, :], raw_scores, -1000000000.0)


def attend_one(items):
    query_one, key_one, value_one, valid_one = items
    scores = masked_scores(query_one, key_one, valid_one)
    top_score = jnp.max(scores, axis=-1, keepdims=True)
    exponent = jnp.exp(scores - top_score)
    row_total = jnp.sum(exponent, axis=-1, keepdims=True)
    log_total = top_score + jnp.log(row_total)
    probs_low = (exponent / row_total).astype(jnp.bfloat16)
    mixed_one = jnp.einsum(
        "hqk,khd->qhd", probs_low, value_one, preferred_element_type=jnp.float32
    ).astype(jnp.bfloat16)
    return (mixed_one, log_total)


def attend_back(items):
    query_one, key_one, value_one, valid_one, log_one, gmix_one = items
    weights_again = jnp.exp(masked_scores(query_one, key_one, valid_one) - log_one)
    g_probs = jnp.einsum("qhd,khd->hqk", gmix_one, value_one, preferred_element_type=jnp.float32)
    inner_sum = jnp.sum(weights_again * g_probs, axis=-1, keepdims=True)
    g_score = (weights_again * (g_probs - inner_sum)).astype(jnp.bfloat16)
    probs_again = weights_again.astype(jnp.bfloat16)
    g_query = (
        jnp.einsum("hqk,khd->qhd", g_score, key_one, preferred_element_type=jnp.float32)
        * HEAD_DIM ** (-0.5)
    ).astype(jnp.bfloat16)
    g_key = jnp.einsum(
        "hqk,qhd->khd", g_score, query_one, preferred_element_type=jnp.float32
    ) * HEAD_DIM ** (-0.5)
    g_value = jnp.einsum("hqk,qhd->khd", probs_again, gmix_one, preferred_element_type=jnp.float32)
    return (g_query, g_key, g_value)


def per_device(
    latents,
    clip_text,
    embedding,
    lengths,
    conv_weight,
    up_weight,
    down_weight,
    hidden_vecs,
    vectors,
    time_weight,
    map_weight,
    attn_in,
    out_weight,
    grad_out,
):
    lat_count, band_rows, columns, channels = latents.shape
    tokens_lat = band_rows * columns
    tok_rows = lat_count * tokens_lat
    hidden_width = up_weight.shape[1]
    text_len = clip_text.shape[1]
    clip_width = clip_text.shape[2]
    band_size = lax.axis_size("band")
    band_index = lax.axis_index("band")
    pixel_count = tokens_lat * band_size
    head_count = channels // HEAD_DIM
    band_share = 1.0 / band_size
    res_shards = (conv_weight, up_weight, down_weight, hidden_vecs, vectors)
    attn_shards = (time_weight, map_weight, attn_in, out_weight)
    res_full = (
        lax.all_gather(res_shards[0], ("dp", "band"), axis=1, tiled=True),
        lax.all_gather(res_shards[1], ("dp", "band"), axis=0, tiled=True),
        lax.all_gather(res_shards[2], ("dp", "band"), axis=0, tiled=True),
        lax.all_gather(res_shards[3], ("dp", "band"), axis=1, tiled=True),
        lax.all_gather(res_shards[4], ("dp", "band"), axis=1, tiled=True),
    )
    attn_full = (
        lax.all_gather(attn_shards[0], ("dp", "band"), axis=1, tiled=True),
        lax.all_gather(attn_shards[1], ("dp", "band"), axis=0, tiled=True),
        lax.all_gather(attn_shards[2], ("dp", "band"), axis=1, tiled=True),
        lax.all_gather(attn_shards[3], ("dp", "band"), axis=0, tiled=True),
    )
    hidden_values = res_full[3].astype(jnp.float32)
    vec_values = res_full[4].astype(jnp.float32)
    framed = with_halo(latents, (("band", 1),), 1)
    framed = jnp.pad(framed, ((0, 0), (0, 0), (1, 1), (0, 0)))
    conv_taps = res_full[0].astype(jnp.float32)
    conv_out = jnp.broadcast_to(vec_values[0], latents.shape)
    for offset in range(9):
        row_shift = offset // 3
        col_shift = offset % 3
        conv_out = conv_out + conv_taps[offset] * framed[
            :, row_shift : row_shift + band_rows, col_shift : col_shift + columns
        ].astype(jnp.float32)
    first_norm, first_inv = norm_parts(conv_out.reshape(tok_rows, channels))
    first_in = first_norm.astype(jnp.bfloat16)
    up_out = product(first_in, res_full[1]) + hidden_values[0]
    active = gelu_exact(up_out)
    active_lat = active.reshape(lat_count, tokens_lat, hidden_width)
    square_sums = lax.psum(
        jnp.sum(active_lat * active_lat, axis=1).astype(jnp.bfloat16), "band"
    ).astype(jnp.float32)
    strength = jnp.sqrt(square_sums)
    grn_denom = jnp.mean(strength, axis=-1, keepdims=True) + 1e-06
    grn_ratio = strength / grn_denom
    gamma_vec = hidden_values[1]
    grn_out = (
        (gamma_vec * (active_lat * grn_ratio[:, None]) + hidden_values[2] + active_lat)
        .astype(jnp.bfloat16)
        .reshape(tok_rows, hidden_width)
    )
    first_sum = latents.reshape(tok_rows, channels).astype(jnp.float32) + (
        product(grn_out, res_full[2]) + vec_values[1]
    )
    modulation = product(embedding, attn_full[0])
    scale_vec = modulation[:, :channels] + vec_values[2]
    shift_vec = modulation[:, channels:] + vec_values[3]
    first_lat = first_sum.reshape(lat_count, tokens_lat, channels)
    second = first_lat * (1.0 + scale_vec[:, None]) + shift_vec[:, None]
    second_norm, second_inv = norm_parts(second)
    second_in = second_norm.astype(jnp.bfloat16).reshape(tok_rows, channels)
    clip_words = (
        jax.nn.silu(clip_text.astype(jnp.float32))
        .astype(jnp.bfloat16)
        .reshape(lat_count * text_len, clip_width)
    )
    mapped = (product(clip_words, attn_full[1]) + vec_values[4]).astype(jnp.bfloat16)
    projections = attn_full[2]
    query_rows = (product(second_in, projections[0]) + vec_values[5]).astype(jnp.bfloat16)
    pixel_key = (
        product(second_in, projections[1])
        .astype(jnp.bfloat16)
        .reshape(lat_count, tokens_lat, channels)
    )
    pixel_value = (
        (product(second_in, projections[2]) + vec_values[6])
        .astype(jnp.bfloat16)
        .reshape(lat_count, tokens_lat, channels)
    )
    all_key, all_value = (
        lax.all_gather(pixel_key, "band", axis=1, tiled=True),
        lax.all_gather(pixel_value, "band", axis=1, tiled=True),
    )
    text_key = (
        product(mapped, projections[1]).astype(jnp.bfloat16).reshape(lat_count, text_len, channels)
    )
    text_value = (
        (product(mapped, projections[2]) + vec_values[6])
        .astype(jnp.bfloat16)
        .reshape(lat_count, text_len, channels)
    )
    key_rows = jnp.concatenate([all_key, text_key], axis=1).reshape(
        lat_count, pixel_count + text_len, head_count, HEAD_DIM
    )
    value_rows = jnp.concatenate([all_value, text_value], axis=1).reshape(
        lat_count, pixel_count + text_len, head_count, HEAD_DIM
    )
    query_heads = query_rows.reshape(lat_count, tokens_lat, head_count, HEAD_DIM)
    key_places = jnp.arange(pixel_count + text_len, dtype=jnp.int32)
    valid_keys = key_places[None, :] < pixel_count + lengths[:, None]
    mixed_heads, log_totals = lax.map(attend_one, (query_heads, key_rows, value_rows, valid_keys))
    mixed_out = mixed_heads.reshape(tok_rows, channels)
    attended = product(mixed_out, attn_full[3]) + vec_values[7]
    layer_out = (
        (second.reshape(tok_rows, channels) + attended).astype(jnp.bfloat16).reshape(latents.shape)
    )
    res_back = (
        lax.all_gather(res_shards[0], ("dp", "band"), axis=1, tiled=True),
        lax.all_gather(res_shards[1], ("dp", "band"), axis=0, tiled=True),
        lax.all_gather(res_shards[2], ("dp", "band"), axis=0, tiled=True),
        lax.all_gather(res_shards[3], ("dp", "band"), axis=1, tiled=True),
        lax.all_gather(res_shards[4], ("dp", "band"), axis=1, tiled=True),
    )
    attn_back = (
        lax.all_gather(attn_shards[0], ("dp", "band"), axis=1, tiled=True),
        lax.all_gather(attn_shards[1], ("dp", "band"), axis=0, tiled=True),
        lax.all_gather(attn_shards[2], ("dp", "band"), axis=1, tiled=True),
        lax.all_gather(attn_shards[3], ("dp", "band"), axis=0, tiled=True),
    )
    proj_back = attn_back[2]
    grad_rows = grad_out.reshape(tok_rows, channels)
    grad_float = grad_rows.astype(jnp.float32)
    out_grad_w = product_tn(mixed_out, grad_rows)
    g_mixed = (
        product_nt(grad_rows, attn_back[3])
        .astype(jnp.bfloat16)
        .reshape(lat_count, tokens_lat, head_count, HEAD_DIM)
    )
    g_query_heads, g_key, g_value = lax.map(
        attend_back, (query_heads, key_rows, value_rows, valid_keys, log_totals, g_mixed)
    )
    g_query = g_query_heads.reshape(tok_rows, channels)
    g_key = g_key.reshape(lat_count, pixel_count + text_len, channels)
    g_value = g_value.reshape(lat_count, pixel_count + text_len, channels)
    pixel_gkey, pixel_gvalue = (
        lax.psum_scatter(
            g_key[:, :pixel_count].astype(jnp.bfloat16), "band", scatter_dimension=1, tiled=True
        ).astype(jnp.float32),
        lax.psum_scatter(
            g_value[:, :pixel_count].astype(jnp.bfloat16), "band", scatter_dimension=1, tiled=True
        ).astype(jnp.float32),
    )
    text_gkey, text_gvalue = (
        lax.psum(g_key[:, pixel_count:].astype(jnp.bfloat16), "band").astype(jnp.float32),
        lax.psum(g_value[:, pixel_count:].astype(jnp.bfloat16), "band").astype(jnp.float32),
    )
    pixel_kb = pixel_gkey.astype(jnp.bfloat16).reshape(tok_rows, channels)
    pixel_vb = pixel_gvalue.astype(jnp.bfloat16).reshape(tok_rows, channels)
    text_kb = text_gkey.astype(jnp.bfloat16).reshape(lat_count * text_len, channels)
    text_vb = text_gvalue.astype(jnp.bfloat16).reshape(lat_count * text_len, channels)
    g_second_in = (
        product_nt(g_query, proj_back[0])
        + product_nt(pixel_kb, proj_back[1])
        + product_nt(pixel_vb, proj_back[2])
    )
    grad_query_w = product_tn(second_in, g_query)
    grad_key_w = product_tn(second_in, pixel_kb) + band_share * product_tn(mapped, text_kb)
    grad_value_w = product_tn(second_in, pixel_vb) + band_share * product_tn(mapped, text_vb)
    g_mapped = (product_nt(text_kb, proj_back[1]) + product_nt(text_vb, proj_back[2])).astype(
        jnp.bfloat16
    )
    grad_map_w = band_share * product_tn(clip_words, g_mapped)
    clip_slice = clip_width // band_size
    map_rows = lax.dynamic_slice_in_dim(attn_back[1], band_index * clip_slice, clip_slice, 0)
    text_part = lax.dynamic_slice_in_dim(clip_text, band_index * clip_slice, clip_slice, 2).astype(
        jnp.float32
    )
    sigmoid_text = jax.nn.sigmoid(text_part)
    g_words = product_nt(g_mapped, map_rows).reshape(lat_count, text_len, clip_slice)
    text_grad = (g_words * (sigmoid_text * (1.0 + text_part * (1.0 - sigmoid_text)))).astype(
        jnp.bfloat16
    )
    g_second = grad_float.reshape(lat_count, tokens_lat, channels) + norm_back(
        g_second_in.reshape(lat_count, tokens_lat, channels), second_norm, second_inv
    )
    g_scale = jnp.sum(g_second * first_lat, axis=1)
    g_shift = jnp.sum(g_second, axis=1)
    grad_time_w = lax.dot_general(
        embedding.astype(jnp.float32),
        jnp.concatenate([g_scale, g_shift], axis=1),
        (((0,), (0,)), ((), ())),
        precision=lax.Precision.HIGHEST,
        preferred_element_type=jnp.float32,
    )
    attn_grads = (
        lax.psum_scatter(grad_time_w, ("dp", "band"), scatter_dimension=1, tiled=True),
        lax.psum_scatter(grad_map_w, ("dp", "band"), scatter_dimension=0, tiled=True),
        lax.psum_scatter(
            jnp.stack([grad_query_w, grad_key_w, grad_value_w]),
            ("dp", "band"),
            scatter_dimension=1,
            tiled=True,
        ),
        lax.psum_scatter(out_grad_w, ("dp", "band"), scatter_dimension=0, tiled=True),
    )
    g_first = g_second * (1.0 + scale_vec[:, None])
    g_down = g_first.astype(jnp.bfloat16).reshape(tok_rows, channels)
    grad_down_w = product_tn(grn_out, g_down)
    g_grn = product_nt(g_down, res_back[2]).reshape(lat_count, tokens_lat, hidden_width)
    grad_gamma = jnp.sum(g_grn * active_lat * grn_ratio[:, None], axis=(0, 1))
    grad_beta = jnp.sum(g_grn, axis=(0, 1))
    g_ratio = lax.psum(
        jnp.sum(g_grn * gamma_vec * active_lat, axis=1).astype(jnp.bfloat16), "band"
    ).astype(jnp.float32)
    g_strength = g_ratio / grn_denom - jnp.sum(g_ratio * strength, axis=-1, keepdims=True) / (
        hidden_width * grn_denom * grn_denom
    )
    g_active = (
        g_grn * (1.0 + gamma_vec * grn_ratio[:, None])
        + active_lat * (g_strength / strength)[:, None]
    )
    gelu_value, gelu_pull = jax.vjp(gelu_exact, up_out)
    g_up = gelu_pull(g_active.reshape(tok_rows, hidden_width))[0].astype(jnp.bfloat16)
    grad_up_w = product_tn(first_in, g_up)
    g_conv = (
        norm_back(product_nt(g_up, res_back[1]), first_norm, first_inv)
        .astype(jnp.bfloat16)
        .reshape(latents.shape)
    )
    g_framed = with_halo(g_conv, (("band", 1),), 1)
    g_framed = jnp.pad(g_framed, ((0, 0), (0, 0), (1, 1), (0, 0)))
    conv_back = res_back[0].astype(jnp.float32)
    g_conv_f = g_conv.astype(jnp.float32)
    back_sum = g_first.reshape(latents.shape)
    tap_grads = []
    for offset in range(9):
        row_shift = offset // 3
        col_shift = offset % 3
        window = framed[
            :, row_shift : row_shift + band_rows, col_shift : col_shift + columns
        ].astype(jnp.float32)
        tap_grads.append(jnp.sum(g_conv_f * window, axis=(0, 1, 2)))
        back_sum = back_sum + conv_back[offset] * g_framed[
            :, 2 - row_shift : 2 - row_shift + band_rows, 2 - col_shift : 2 - col_shift + columns
        ].astype(jnp.float32)
    latent_grad = back_sum.astype(jnp.bfloat16)
    grad_vectors = jnp.stack(
        [
            jnp.sum(g_conv_f, axis=(0, 1, 2)),
            column_sums(g_down),
            jnp.sum(g_scale, axis=0),
            jnp.sum(g_shift, axis=0),
            band_share * column_sums(g_mapped),
            column_sums(g_query),
            column_sums(pixel_vb) + band_share * column_sums(text_vb),
            jnp.sum(grad_float, axis=0),
        ]
    )
    grad_hidden = jnp.stack([column_sums(g_up), grad_gamma, grad_beta])
    grad_conv_w = jnp.stack(tap_grads)
    res_grads = (
        lax.psum_scatter(grad_conv_w, ("dp", "band"), scatter_dimension=1, tiled=True),
        lax.psum_scatter(grad_up_w, ("dp", "band"), scatter_dimension=0, tiled=True),
        lax.psum_scatter(grad_down_w, ("dp", "band"), scatter_dimension=0, tiled=True),
        lax.psum_scatter(grad_hidden, ("dp", "band"), scatter_dimension=1, tiled=True),
        lax.psum_scatter(grad_vectors, ("dp", "band"), scatter_dimension=1, tiled=True),
    )
    return (
        layer_out,
        latent_grad,
        text_grad,
        res_grads[0],
        res_grads[1],
        res_grads[2],
        res_grads[3],
        res_grads[4],
        attn_grads[0],
        attn_grads[1],
        attn_grads[2],
        attn_grads[3],
    )


PLANE = 4
LINE = 4
PAIR = 2 * HEAD_DIM


def key_bias(length, keys, pixels):
    rows = lax.broadcasted_iota(jnp.int32, (keys, 1), 0)
    return jnp.where(rows < pixels + length, 0.0, -1000000000.0)


def one_head(value, head):
    lanes = lax.broadcasted_iota(jnp.int32, value.shape, 1)
    return jnp.where((lanes // HEAD_DIM) == head, value, jnp.zeros_like(value))


def attend_kernel(pixels, length_ref, rows_ref, mixed_ref, log_ref):
    keys = rows_ref.shape[1]
    bias = key_bias(length_ref[pl.program_id(0)], keys, pixels)
    query = rows_ref[0, :pixels, :PAIR] * HEAD_DIM ** (-0.5)
    key = rows_ref[0, :, PAIR : 2 * PAIR]
    value = rows_ref[0, :, 2 * PAIR :]
    total = jnp.zeros((pixels, PAIR), jnp.float32)
    for head in range(PAIR // HEAD_DIM):
        scores = product_nt(key, one_head(query, head)) + bias
        top = jnp.max(scores, axis=0, keepdims=True)
        exponent = jnp.exp(scores - top)
        row_total = jnp.sum(exponent, axis=0, keepdims=True)
        probs = (exponent * (1.0 / row_total)).astype(jnp.bfloat16)
        total = total + product_tn(probs, one_head(value, head))
        log_ref[0, 0, head : head + 1, :] = top + jnp.log(row_total)
    mixed_ref[0] = total.astype(jnp.bfloat16)


def attend_back_kernel(pixels, length_ref, rows_ref, gmix_ref, log_ref, grad_ref):
    keys = rows_ref.shape[1]
    bias = key_bias(length_ref[pl.program_id(0)], keys, pixels)
    query = rows_ref[0, :pixels, :PAIR] * HEAD_DIM ** (-0.5)
    key = rows_ref[0, :, PAIR : 2 * PAIR]
    value = rows_ref[0, :, 2 * PAIR :]
    g_query = jnp.zeros((pixels, PAIR), jnp.float32)
    g_key = jnp.zeros((keys, PAIR), jnp.float32)
    g_value = jnp.zeros((keys, PAIR), jnp.float32)
    for head in range(PAIR // HEAD_DIM):
        query_one = one_head(query, head)
        gmix_one = one_head(gmix_ref[0], head)
        scores = product_nt(key, query_one) + bias
        weights = jnp.exp(scores - log_ref[0, 0, head : head + 1, :])
        g_probs = product_nt(value, gmix_one)
        inner = jnp.sum(weights * g_probs, axis=0, keepdims=True)
        g_score = (weights * (g_probs - inner)).astype(jnp.bfloat16)
        g_key = g_key + product(g_score, query_one)
        g_value = g_value + product(weights.astype(jnp.bfloat16), gmix_one)
        g_query = g_query + product_tn(g_score, one_head(key, head))
    g_query = (g_query * HEAD_DIM ** (-0.5)).astype(jnp.bfloat16)
    grad_ref[0, :pixels, :PAIR] = g_query
    grad_ref[0, pixels:, :PAIR] = jnp.zeros((keys - pixels, PAIR), jnp.bfloat16)
    grad_ref[0, :, PAIR : 2 * PAIR] = g_key.astype(jnp.bfloat16)
    grad_ref[0, :, 2 * PAIR :] = g_value.astype(jnp.bfloat16)


def attend_specs(keys, pixels):
    rows = pl.BlockSpec((1, keys, 3 * PAIR), lambda i, j, n: (i, 0, j))
    narrow = pl.BlockSpec((1, pixels, PAIR), lambda i, j, n: (i, 0, j))
    logs = pl.BlockSpec((1, 1, PAIR // HEAD_DIM, pixels), lambda i, j, n: (i, j, 0, 0))
    return (rows, narrow, logs)


def attend(rows, lengths, pixels):
    count, keys, width = rows.shape
    groups = width // (3 * PAIR)
    rows_spec, narrow, logs = attend_specs(keys, pixels)
    return pl.pallas_call(
        functools.partial(attend_kernel, pixels),
        out_shape=(
            jax.ShapeDtypeStruct((count, pixels, groups * PAIR), jnp.bfloat16),
            jax.ShapeDtypeStruct((count, groups, PAIR // HEAD_DIM, pixels), jnp.float32),
        ),
        grid_spec=pltpu.PrefetchScalarGridSpec(
            num_scalar_prefetch=1,
            grid=(count, groups),
            in_specs=[rows_spec],
            out_specs=[narrow, logs],
        ),
        compiler_params=pltpu.CompilerParams(vmem_limit_bytes=40 << 20),
        cost_estimate=pl.CostEstimate(
            flops=count * groups * 8 * pixels * keys * PAIR,
            bytes_accessed=rows.size * 3,
            transcendentals=2 * count * groups * pixels * keys,
        ),
        name="attend",
    )(lengths, rows)


def attend_back_pairs(rows, g_mixed, logs_in, lengths, pixels):
    count, keys, width = rows.shape
    groups = width // (3 * PAIR)
    rows_spec, narrow, logs = attend_specs(keys, pixels)
    return pl.pallas_call(
        functools.partial(attend_back_kernel, pixels),
        out_shape=jax.ShapeDtypeStruct(rows.shape, jnp.bfloat16),
        grid_spec=pltpu.PrefetchScalarGridSpec(
            num_scalar_prefetch=1,
            grid=(count, groups),
            in_specs=[rows_spec, narrow, logs],
            out_specs=rows_spec,
        ),
        compiler_params=pltpu.CompilerParams(vmem_limit_bytes=40 << 20),
        cost_estimate=pl.CostEstimate(
            flops=count * groups * 20 * pixels * keys * PAIR,
            bytes_accessed=rows.size * 5,
            transcendentals=2 * count * groups * pixels * keys,
        ),
        name="attend_back",
    )(lengths, rows, g_mixed, logs_in)


def swap(value, bit):
    return lax.ppermute(value, "dp", [(i, i ^ bit) for i in range(2 * PLANE)])


def rotate(value, step):
    return lax.ppermute(value, "band", [(i, (i + step) % LINE) for i in range(LINE)])


def pick(value, index, axis=0):
    return lax.dynamic_index_in_dim(value, index, axis, keepdims=False)


def put(buffer, value, index, axis=0):
    return lax.dynamic_update_index_in_dim(buffer, value, index, axis)


def spread_line(blocks, place):
    result = jnp.zeros(blocks.shape, blocks.dtype)
    result = put(result, pick(blocks, place), place)
    for step in range(1, LINE):
        moved = rotate(pick(blocks, (place + step) % LINE), step)
        result = put(result, moved, (place - step) % LINE)
    return result


def gather_line(shard, place):
    parts, rows, cols = shard.shape
    result = jnp.zeros((parts, LINE, rows, cols), shard.dtype)
    result = put(result, shard, place, 1)
    for step in range(1, LINE):
        result = put(result, rotate(shard, step), (place - step) % LINE, 1)
    return result


def gather_plane(block, plane):
    rows, cols = block.shape
    half = rows // 2
    by_x, by_y = (swap(block, 2), swap(block, 4))
    upper = swap(by_y[:half], 2)
    lower = swap(by_x[half:], 4)
    result = jnp.zeros((PLANE, rows, cols), block.dtype)
    result = put(result, block, plane)
    result = put(result, by_x, plane ^ 1)
    result = put(result, by_y, plane ^ 2)
    zero = jnp.int32(0)
    result = lax.dynamic_update_slice(result, upper[None], (plane ^ 3, zero, zero))
    result = lax.dynamic_update_slice(result, lower[None], (plane ^ 3, zero + half, zero))
    return (result, (by_x, by_y))


def held(*values):
    return lax.optimization_barrier(values)


def flat_line(shard, place):
    parts, rows, cols = shard.shape
    return gather_line(shard, place).reshape(parts * LINE * rows, cols)


def flat_plane(line, plane):
    full, _ = gather_plane(line, plane)
    return full.reshape(-1, line.shape[1])


def reduce_owner(pieces, parts, plane, place):
    low, f32 = (jnp.bfloat16, jnp.float32)
    first, second, last = pieces
    far = first(plane ^ 3).astype(low)
    half = far.shape[1] // 2
    via_x, via_y = (swap(far[:, :half], 2), swap(far[:, half:], 4))
    left = jnp.pad(via_x.astype(f32), ((0, 0), (0, half)))
    right = jnp.pad(via_y.astype(f32), ((0, 0), (half, 0)))
    got_x = swap((second(plane ^ 1) + right).astype(low), 2)
    got_y = swap((second(plane ^ 2) + left).astype(low), 4)
    total = last(plane) + got_x.astype(f32) + got_y.astype(f32)
    rows, cols = total.shape
    shaped = total.reshape(parts, LINE, rows // (parts * LINE), cols)
    summed = pick(shaped, place, 1)
    for step in range(1, LINE):
        sent = pick(shaped, (place + step) % LINE, 1).astype(low)
        summed = summed + rotate(sent, step).astype(f32)
    return (summed, total)


def gather_small(value, plane, core, place):
    cores = jnp.zeros((2,) + value.shape, value.dtype)
    cores = put(put(cores, value, core), swap(value, 1), 1 - core)
    full = gather_small_plane(cores, plane)
    line = jnp.zeros((LINE,) + full.shape, value.dtype)
    line = put(line, full, place)
    for step in range(1, LINE):
        line = put(line, rotate(full, step), (place - step) % LINE)
    return line


def gather_small_plane(line, plane):
    by_x = swap(line, 2)
    both = jnp.stack([line, by_x])
    by_y = swap(both, 4)
    full = jnp.zeros((PLANE,) + line.shape, line.dtype)
    full = put(put(full, line, plane), by_x, plane ^ 1)
    return put(put(full, by_y[0], plane ^ 2), by_y[1], plane ^ 3)


def reduce_small(value, plane, place):
    both = jnp.stack([pick(value, plane ^ 1), pick(value, plane ^ 3)])
    by_x = swap(both, 2)
    mine = pick(value, plane) + by_x[0]
    other = pick(value, plane ^ 2) + by_x[1]
    mine = mine + swap(other, 4)
    summed = pick(mine, place)
    for step in range(1, LINE):
        summed = summed + rotate(pick(mine, (place + step) % LINE), step)
    return summed


def pair(value):
    return jnp.stack([value, swap(value, 1)])


def pair_sum(value):
    return value + swap(value, 1)[::-1]


def own_sum(own, partner):
    return own + swap(partner.astype(jnp.bfloat16), 1).astype(jnp.float32)


def core_half(value, axis, core, chips=PLANE):
    shape = value.shape
    split = shape[:axis] + (chips, 2, shape[axis] // (2 * chips)) + shape[axis + 1 :]
    half = pick(value.reshape(split), core, axis + 1)
    return half.reshape(shape[:axis] + (shape[axis] // 2,) + shape[axis + 1 :])


def core_merge(own, other, axis, core):
    shape = own.shape
    split = shape[:axis] + (PLANE, 1, shape[axis] // PLANE) + shape[axis + 1 :]
    own, other = (own.reshape(split), other.reshape(split))
    first = jnp.where(core == 0, own, other)
    second = jnp.where(core == 0, other, own)
    merged = jnp.concatenate([first, second], axis=axis + 1)
    return merged.reshape(shape[:axis] + (2 * shape[axis],) + shape[axis + 1 :])


def paired_device(
    latents,
    clip_text,
    embedding,
    lengths,
    conv_weight,
    up_weight,
    down_weight,
    hidden_vecs,
    vectors,
    time_weight,
    map_weight,
    attn_in,
    out_weight,
    grad_out,
):
    lat_count, band_rows, columns, channels = latents.shape
    height = band_rows * LINE
    pixels = height * columns
    text_len, clip_width = clip_text.shape[1:]
    hidden_width = up_weight.shape[1]
    time_rank = time_weight.shape[0]
    half_channels, half_hidden = (channels // 2, hidden_width // 2)
    dp_index = lax.axis_index("dp")
    place = lax.axis_index("band")
    plane, core = (dp_index // 2, dp_index % 2)
    f32, low = (jnp.float32, jnp.bfloat16)

    small = jnp.concatenate(
        [
            conv_weight.reshape(-1),
            vectors.reshape(-1),
            hidden_vecs.reshape(-1),
            time_weight.reshape(-1),
        ]
    )
    small_low = gather_small(small, plane, core, place)
    small_all = small_low.astype(f32)
    time_at = small.size - time_weight.size
    col_rows, col_width = (9 + vectors.shape[0], conv_weight.shape[1])
    col_all = small_all[..., : col_rows * col_width]
    col_all = col_all.reshape(LINE, PLANE, 2, col_rows, col_width).transpose(3, 1, 2, 0, 4)
    col_all = col_all.reshape(col_rows, channels)
    taps, vecs = (col_all[:9], col_all[9:])
    hidden_all = pick(small_all[..., col_rows * col_width : time_at], core, 2)
    hidden_all = hidden_all.reshape(LINE, PLANE, 3, -1).transpose(2, 1, 0, 3)
    hidden_all = hidden_all.reshape(3, half_hidden)

    def with_partner(value, axis):
        kept = core_half(value, axis, core)
        got = swap(core_half(value, axis, 1 - core), 1)
        both = jnp.zeros((2,) + kept.shape, kept.dtype)
        return put(put(both, kept, core), got, 1 - core)

    def attn_order(value):
        groups = jnp.moveaxis(value.reshape(value.shape[:-1] + (-1, PAIR)), 0, -2)
        return groups.reshape(groups.shape[:-3] + (-1,))

    def attn_back_order(value):
        groups = jnp.moveaxis(value.reshape(value.shape[:-1] + (-1, 3, PAIR)), -2, 0)
        return groups.reshape(groups.shape[:-2] + (-1,))

    up_shard = with_partner(up_weight, 1)
    attn_shard = attn_order(jnp.moveaxis(with_partner(attn_in, 2), 1, 0))

    latent = spread_line(latents, place).reshape(height, columns, channels)
    up_line = flat_line(up_shard, place)
    up_line, latent, down_shard, map_shard, time_low = held(
        up_line, latent, down_weight[None], map_weight[None], small_low[..., time_at:]
    )
    up_full = flat_plane(up_line, plane)
    down_line = flat_line(down_shard, place)
    map_line = flat_line(map_shard, place)
    time_all = time_low.reshape(LINE, PLANE, 2, time_rank, -1).transpose(3, 1, 2, 0, 4)
    time_all = time_all.reshape(time_rank, 2 * channels)
    clip_own = pick(clip_text, place).astype(f32)
    words_own = jax.nn.silu(clip_own).astype(low)
    text_pad = -(-text_len // 16) * 16
    words_own = jnp.pad(words_own, ((0, text_pad - text_len), (0, 0)))
    words = pair(words_own).reshape(2 * text_pad, clip_width)
    words_half = core_half(words, 1, core)
    lengths_two = pair(pick(lengths, place))
    embed_own = pick(embedding, place)

    framed = jnp.pad(latent, ((1, 1), (1, 1), (0, 0)))
    conv_out = jnp.broadcast_to(vecs[0], latent.shape)
    for offset in range(9):
        row_shift, col_shift = (offset // 3, offset % 3)
        conv_out = conv_out + taps[offset] * framed[
            row_shift : row_shift + height, col_shift : col_shift + columns
        ].astype(f32)
    first_norm, first_inv = norm_parts(conv_out.reshape(pixels, channels))
    first_in = pair(first_norm.astype(low)).reshape(2 * pixels, channels)
    up_full, down_line, map_line, first_in, words_half, attn_shard = held(
        up_full, down_line, map_line, first_in, words_half, attn_shard
    )
    down_full = flat_plane(down_line, plane)
    map_full = flat_plane(map_line, plane)
    attn_line = flat_line(attn_shard, place)
    up_out = product(first_in, up_full) + hidden_all[0]
    below = 0.5 + 0.5 * lax.erf(up_out * 0.5**0.5)
    slope = below + up_out * ((0.5 / jnp.pi) ** 0.5 * jnp.exp(-0.5 * up_out * up_out))
    active, slope = held((up_out * below).astype(low), slope.astype(low))
    active_lat = active.reshape(2, pixels, half_hidden).astype(f32)
    strength = jnp.sqrt(jnp.sum(active_lat * active_lat, axis=1))
    strength_sum = pair_sum(jnp.sum(strength, axis=-1, keepdims=True))
    grn_denom = strength_sum / hidden_width + 1e-06
    grn_ratio = strength / grn_denom
    gamma_vec = hidden_all[1]
    grn_out = (
        gamma_vec * (active_lat * grn_ratio[:, None]) + hidden_all[2] + active_lat
    ).astype(low)
    grn_out, down_full, map_full, attn_line, out_shard = held(
        grn_out, down_full, map_full, attn_line, out_weight[None]
    )
    attn_full = flat_plane(attn_line, plane)
    out_line = flat_line(out_shard, place)
    lowered = own_sum(product(grn_out[0], down_full), product(grn_out[1], down_full))
    first_sum = latent.reshape(pixels, channels).astype(f32) + (lowered + vecs[1])
    modulation = product(embed_own[None], time_all)[0]
    scale_vec = modulation[:channels] + vecs[2]
    shift_vec = modulation[channels:] + vecs[3]
    second = first_sum * (1.0 + scale_vec) + shift_vec
    second_norm, second_inv = norm_parts(second)
    mapped = pair_sum(product(words_half, map_full).reshape(2, text_pad, channels))
    mapped = (mapped + vecs[4]).astype(low)
    sources = jnp.concatenate([pair(second_norm.astype(low)), mapped], axis=1)
    keys = pixels + text_pad
    sources, attn_full, out_line, grad_shard = held(sources, attn_full, out_line, grad_out)
    sources = sources.reshape(2 * keys, channels)
    out_full = flat_plane(out_line, plane)
    grad_own = spread_line(grad_shard, place).reshape(pixels, channels)
    bias = jnp.stack([vecs[5], jnp.zeros((channels,), f32), vecs[6]])
    bias = attn_order(core_half(bias, 1, core))
    rows_qkv = (product(sources, attn_full) + bias).astype(low)
    rows_qkv = rows_qkv.reshape(2, keys, 3 * half_channels)
    mixed, log_totals = attend(rows_qkv, lengths_two, pixels)
    attended = own_sum(product(mixed[0], out_full), product(mixed[1], out_full))
    layer_own = (second + (attended + vecs[7])).astype(low)
    grad_two = pair(grad_own)
    g_mixed = product_nt(grad_two.reshape(2 * pixels, channels), out_full).astype(low)
    g_mixed = g_mixed.reshape(2, pixels, half_channels)

    def owner_sums(left, right, parts, *gates):
        block = left.shape[1] // PLANE

        def pieces_of(left_op, right_op):
            def piece(chip):
                taken = lax.dynamic_slice_in_dim(left_op, chip * block, block, 1)
                return product_tn(taken, right_op)

            return piece

        pieces = [pieces_of(left, right)]
        for gate in gates:
            left, right, _ = held(left, right, gate)
            pieces.append(pieces_of(left, right))
        pieces += [pieces[-1]] * (3 - len(pieces))
        return reduce_owner(pieces, parts, plane, place)

    g_rows = attend_back_pairs(rows_qkv, g_mixed, log_totals, lengths_two, pixels)
    layer_out = spread_line(layer_own.reshape(latents.shape), place)
    g_rows, layer_out = held(g_rows, layer_out)
    g_second_in = own_sum(
        product_nt(g_rows[0, :pixels], attn_full), product_nt(g_rows[1, :pixels], attn_full)
    )
    out_grad = owner_sums(
        mixed.reshape(2 * pixels, half_channels),
        grad_two.reshape(2 * pixels, channels),
        1,
        g_rows,
        g_second_in,
    )[0][0]
    g_second_in, g_rows = held(g_second_in, g_rows)
    g_flat = g_rows.reshape(2 * keys, 3 * half_channels)
    grad_float = grad_own.astype(f32)
    g_second = grad_float + norm_back(g_second_in, second_norm, second_inv)
    g_scale = jnp.sum(g_second * first_sum, axis=0)
    g_shift = jnp.sum(g_second, axis=0)
    g_modulation = jnp.concatenate([g_scale, g_shift])
    time_part = embed_own.astype(f32)[:, None] * g_modulation[None]
    g_first = g_second * (1.0 + scale_vec)
    g_down_own = g_first.astype(low)
    g_down = pair(g_down_own).reshape(2 * pixels, channels)
    g_grn = product_nt(g_down, down_full).reshape(2, pixels, half_hidden)
    g_grn_active = jnp.sum(g_grn * active_lat, axis=1)
    g_grn_sum = jnp.sum(g_grn, axis=(0, 1))
    g_grn, g_grn_active, grad_beta = held(g_grn.astype(low), g_grn_active, g_grn_sum)
    g_grn_low = g_grn
    g_grn = g_grn.astype(f32)
    grad_gamma = jnp.sum(g_grn_active * grn_ratio, axis=0)
    g_ratio = g_grn_active * gamma_vec
    ratio_sum = pair_sum(jnp.sum(g_ratio * strength, axis=-1, keepdims=True))
    g_strength = g_ratio / grn_denom - ratio_sum / (hidden_width * grn_denom * grn_denom)
    g_active = (
        g_grn * (1.0 + gamma_vec * grn_ratio[:, None])
        + active_lat * (g_strength / strength)[:, None]
    )
    g_up = (g_active.reshape(2 * pixels, half_hidden) * slope.astype(f32)).astype(low)
    attn_grad, _ = owner_sums(sources, g_flat, 2, g_down, g_grn_low)
    down_grad = owner_sums(
        grn_out.reshape(2 * pixels, half_hidden), g_down, 1, g_grn_low, g_up
    )[0][0]
    g_text, _ = held(g_rows[:, pixels:], g_down)
    g_text = g_text.reshape(2 * text_pad, 3 * half_channels)
    g_mapped = pair_sum(product_nt(g_text, attn_full).reshape(2, text_pad, channels))
    g_mapped = g_mapped.astype(low).reshape(2 * text_pad, channels)
    map_grad = owner_sums(words_half, g_mapped, 1, g_grn_low, g_up)[0][0]
    g_words = product_nt(g_mapped, map_full).reshape(2, text_pad, -1)[:, :text_len]
    g_words = core_merge(g_words[0], swap(g_words[1], 1), 1, core)
    sigmoid_text = jax.nn.sigmoid(clip_own)
    text_own = (g_words * (sigmoid_text * (1.0 + clip_own * (1.0 - sigmoid_text)))).astype(low)
    text_own = text_own.reshape(text_len, LINE, clip_width // LINE).transpose(1, 0, 2)
    text_grad = spread_line(text_own, place)
    g_first_in = own_sum(
        product_nt(g_up[:pixels], up_full), product_nt(g_up[pixels:], up_full)
    )
    g_conv = norm_back(g_first_in, first_norm, first_inv).astype(low).reshape(latent.shape)
    up_grad, up_total = owner_sums(first_in, g_up, 2, g_conv)
    g_framed = jnp.pad(g_conv, ((1, 1), (1, 1), (0, 0)))
    g_conv_f = g_conv.astype(f32)
    back_sum = g_first.reshape(latent.shape)
    tap_grads = []
    for offset in range(9):
        row_shift, col_shift = (offset // 3, offset % 3)
        window = framed[
            row_shift : row_shift + height, col_shift : col_shift + columns
        ].astype(f32)
        tap_grads.append(jnp.sum(g_conv_f * window, axis=(0, 1)))
        back_sum = back_sum + taps[offset] * g_framed[
            2 - row_shift : 2 - row_shift + height, 2 - col_shift : 2 - col_shift + columns
        ].astype(f32)
    latent_grad = spread_line(back_sum.astype(low).reshape(latents.shape), place)

    up_grad = core_merge(
        pick(up_grad, core), swap(pick(up_grad, 1 - core), 1), 1, core
    )
    attn_grad = core_merge(
        attn_back_order(pick(attn_grad, core)),
        attn_back_order(swap(pick(attn_grad, 1 - core), 1)),
        2,
        core,
    )
    column_grads = attn_back_order(column_sums(g_flat))
    own_zero = jnp.zeros((half_channels,), f32)
    vec_parts = jnp.stack(
        [
            jnp.sum(g_conv_f, axis=(0, 1)),
            column_sums(g_down_own),
            g_scale,
            g_shift,
            column_sums(g_mapped[:text_pad]),
            core_merge(column_grads[0], own_zero, 0, core),
            core_merge(column_grads[2], own_zero, 0, core),
            jnp.sum(grad_float, axis=0),
        ]
    )
    col_parts = jnp.concatenate([jnp.stack(tap_grads), vec_parts])
    col_parts = col_parts.reshape(col_parts.shape[0], PLANE, 2, LINE, -1).transpose(1, 2, 3, 0, 4)
    col_parts = col_parts.reshape(PLANE, 2, LINE, -1)
    time_part = time_part.reshape(time_rank, PLANE, 2, LINE, -1).transpose(1, 2, 3, 0, 4)
    time_part = time_part.reshape(PLANE, 2, LINE, -1)
    core_parts = jnp.concatenate([col_parts, time_part], axis=-1)
    core_parts, _ = held(core_parts, up_total)
    core_sum = pick(core_parts, core, 1) + swap(pick(core_parts, 1 - core, 1), 1)
    hidden_parts = jnp.stack([column_sums(g_up), grad_gamma, grad_beta])
    hidden_parts = hidden_parts.reshape(3, PLANE, LINE, -1).transpose(1, 2, 0, 3)
    hidden_parts = hidden_parts.reshape(PLANE, LINE, -1)
    small_sum = reduce_small(
        jnp.concatenate([core_sum, hidden_parts], axis=-1), plane, place
    )
    col_size, time_size = (17 * (channels // 32), time_rank * (channels // 16))
    col_grads = small_sum[:col_size].reshape(17, -1)
    time_grad = small_sum[col_size : col_size + time_size].reshape(time_rank, -1)
    hidden_grad = small_sum[col_size + time_size :].reshape(3, -1)
    return (
        layer_out,
        latent_grad,
        text_grad,
        col_grads[:9],
        up_grad,
        down_grad,
        hidden_grad,
        col_grads[9:],
        time_grad,
        map_grad,
        attn_grad,
        out_grad,
    )


def choose(latents, *rest):
    shape = {axis: lax.axis_size(axis) for axis in ("dp", "band")}
    fits = (
        shape["dp"] == 2 * PLANE
        and shape["band"] == LINE
        and latents.shape[0] == LINE
        and latents.shape[3] % (2 * PLANE * HEAD_DIM) == 0
    )
    return (paired_device if fits else per_device)(latents, *rest)


def solution(mesh):
    placed = (
        P("dp", "band", None, None),
        P("dp", None, None),
        P("dp", None),
        P("dp"),
        P(None, ("dp", "band")),
        P(("dp", "band"), None),
        P(("dp", "band"), None),
        P(None, ("dp", "band")),
        P(None, ("dp", "band")),
        P(None, ("dp", "band")),
        P(("dp", "band"), None),
        P(None, ("dp", "band"), None),
        P(("dp", "band"), None),
        P("dp", "band", None, None),
    )
    return jax.shard_map(
        choose,
        mesh=mesh,
        in_specs=placed,
        out_specs=(
            P("dp", "band", None, None),
            P("dp", "band", None, None),
            P("dp", None, "band"),
            P(None, ("dp", "band")),
            P(("dp", "band"), None),
            P(("dp", "band"), None),
            P(None, ("dp", "band")),
            P(None, ("dp", "band")),
            P(None, ("dp", "band")),
            P(("dp", "band"), None),
            P(None, ("dp", "band"), None),
            P(("dp", "band"), None),
        ),
        check_vma=False,
    )
```
